32 devices in a mesh: energy: 8 (over y, x, core), cuts: 4 (over z).
Axes of the slice: x: 2, y: 2, z: 4, core: 2. Of those that a mesh axis runs over, the one named last changes fastest.
Arguments:
- green_diag: bfloat16 [4, 32, 2, 256, 256], P('cuts', 'energy'), may hold values from -0.375 to 0.375
- green_upper: bfloat16 [4, 32, 2, 256, 256], P('cuts', 'energy'), may hold values from -0.375 to 0.375
- sigma_lesser: bfloat16 [4, 32, 2, 256, 256], P('cuts', 'energy'), may hold values from -6 to 6
- screening: bfloat16 [4, 32, 2, 256, 256], P('cuts', 'energy'), may hold values from -0.375 to 0.375
Outputs:
- polar_screened: bfloat16 [4, 32, 2, 256, 256], P('cuts', 'energy')
The draws below stay inside these ranges and needn't reach their ends.
All inputs are finite; a program needn't handle non-finite values.
Results may differ from the reference program's by a relative error of at most 0.013.
Values may be sent and summed in bfloat16 or wider, within the bound.
A program may use at most 64 MiB of HBM per device.

```python
import jax
import jax.numpy as jnp
from jax import lax

B = 256
NE = 32
SLICES = 4
PAD = 64


def shard_levels(own_key, dims, cuts, least, top_value):
    def one(dim, blocks):
        steps = jax.random.uniform(jax.random.fold_in(jax.random.fold_in(own_key, 6), dim), (blocks,), jnp.float32, least / len(cuts), top_value / len(cuts))
        return jnp.repeat(jnp.exp(steps), dims[dim] // blocks).reshape((-1,) + (1,) * (len(dims) - dim - 1))

    loudness = one(*cuts[0])
    for cut in cuts[1:]:
        loudness = loudness * one(*cut)
    return loudness


def centred(rng, extent, spread, most, split=(), dtype=jnp.bfloat16):
    gain = shard_levels(rng, extent, split, -0.22, 0.18) if split else 1.0
    array = jax.random.normal(rng, extent, jnp.float32) * spread * gain
    return jnp.minimum(jnp.maximum(array, -most), most).astype(dtype)


def setup_inputs(seed: int = 0) -> dict:
    arg_keys = jax.random.split(jax.random.key(seed), 5)
    return {
        "green_diag": centred(arg_keys[0], (SLICES, NE, 2, B, B), B ** -0.5, 0.375, ((0, 4), (1, 8))),
        "green_upper": centred(arg_keys[1], (SLICES, NE, 2, B, B), B ** -0.5, 0.375, ((0, 4), (1, 8))),
        "sigma_lesser": centred(arg_keys[2], (SLICES, NE, 2, B, B), 1.0, 6.0, ((0, 4), (1, 8))),
        "screening": centred(arg_keys[3], (SLICES, NE, 2, B, B), B ** -0.5, 0.375, ((0, 4), (1, 8))),
    }


def times_block(left, right):
    left = left.astype(jnp.float32)
    right = right.astype(jnp.float32)
    real = jnp.einsum('eij,ejk->eik', left[:, 0], right[:, 0]) - jnp.einsum('eij,ejk->eik', left[:, 1], right[:, 1])
    imag = jnp.einsum('eij,ejk->eik', left[:, 0], right[:, 1]) + jnp.einsum('eij,ejk->eik', left[:, 1], right[:, 0])
    return jnp.stack([real, imag], axis=1)


def times_adjoint(left, right):
    left = left.astype(jnp.float32)
    right = right.astype(jnp.float32)
    real = jnp.einsum('eij,ekj->eik', left[:, 0], right[:, 0]) + jnp.einsum('eij,ekj->eik', left[:, 1], right[:, 1])
    imag = jnp.einsum('eij,ekj->eik', left[:, 1], right[:, 0]) - jnp.einsum('eij,ekj->eik', left[:, 0], right[:, 1])
    return jnp.stack([real, imag], axis=1)


def one_slice(inputs):
    green_diag, green_upper, sigma_here, sigma_after, screening = inputs
    own_term = times_block(green_diag, sigma_here).astype(jnp.bfloat16)
    pair_term = times_block(green_upper, sigma_after).astype(jnp.bfloat16)
    lesser = (times_adjoint(own_term, green_diag) + times_adjoint(pair_term, green_upper)).astype(jnp.bfloat16)
    values = lesser.astype(jnp.float32)
    signal = lax.complex(values[:, 0], values[:, 1])
    spectrum = jnp.fft.fft(signal, n=PAD, axis=0)
    power = jnp.real(spectrum) ** 2 + jnp.imag(spectrum) ** 2
    lagged = jnp.fft.ifft(power, axis=0)[:NE]
    polar = (jnp.stack([jnp.real(lagged), jnp.imag(lagged)], axis=1) / NE).astype(jnp.bfloat16)
    screened_left = times_block(screening, polar).astype(jnp.bfloat16)
    return times_adjoint(screened_left, screening).astype(jnp.bfloat16)


def reference(green_diag, green_upper, sigma_lesser, screening):
    sigma_next = jnp.concatenate([sigma_lesser[1:], jnp.zeros_like(sigma_lesser[:1])], axis=0)
    return lax.map(one_slice, (green_diag, green_upper, sigma_lesser, sigma_next, screening))
```

```python
import functools
import math

import jax
import jax.numpy as jnp
from jax import lax
from jax.experimental import pallas as pl
from jax.experimental.pallas import tpu as pltpu
from jax.sharding import PartitionSpec as P

LANES = 128
SUB = 8
SHARE = 4
MESH = pl.DeviceIdType.MESH
F32 = jnp.float32
BF16 = jnp.bfloat16


def fill_tables(fwd_ref, inv_ref, groups, local):
    width = 2 * groups
    period = width * local

    def index(shape, axis, unit, count):
        return lax.rem(lax.div(lax.broadcasted_iota(jnp.int32, shape, axis), unit), count)

    def table(shape, phase, quarters, scale):
        turn = lax.rem(phase + quarters * (period // 4), period)
        value = jnp.cos(turn.astype(F32) * (2.0 * math.pi / period)) * scale
        same = index(shape, 0, 1, SUB) == index(shape, 1, 1, SUB)
        return jnp.where(same, value, 0.0).astype(BF16)

    for j in range(local):
        shape = fwd_ref.shape[1:]
        point = index(shape, 0, SUB, width)
        turn = index(shape, 0, SUB * width, 2) - index(shape, 1, SUB, 2) + 4
        energy = index(shape, 1, 2 * SUB, groups) * local + j
        fwd_ref[j] = table(shape, lax.rem(point * energy, period), turn, 1.0)

        shape = inv_ref.shape[1:]
        component = index(shape, 0, SUB, 2)
        part = index(shape, 1, SUB * width, 2)
        lag = index(shape, 0, 2 * SUB, groups) * local + j
        other = 1 - component if 2 * j <= local else 3 - component
        turn = jnp.where(part == 0, 3 * component, other)
        point = index(shape, 1, SUB, width)
        inv_ref[j] = table(shape, lax.rem(point * lag, period), turn, 2.0 / period / period)


def negated(x):
    return None if x is None else -x


def scaled(x, factor):
    return None if x is None else x * factor


def turned(value, numerator, denominator):
    re, im = value
    angle = numerator % denominator
    if angle == 0:
        return re, im
    if 2 * angle == denominator:
        return negated(re), negated(im)
    if 4 * angle == denominator:
        return negated(im), re
    if 4 * angle == 3 * denominator:
        return im, negated(re)
    c = math.cos(2.0 * math.pi * angle / denominator)
    s = math.sin(2.0 * math.pi * angle / denominator)
    return added((scaled(re, c), scaled(re, s)), (scaled(im, -s), scaled(im, c)))


def added(left, right):
    def one(x, y):
        return y if x is None else x if y is None else x + y

    return one(left[0], right[0]), one(left[1], right[1])


def short_transform(values, sign):
    count = len(values)
    if count == 1:
        return values
    if count % 2:
        result = []
        for m in range(count):
            total = values[0]
            for j in range(1, count):
                total = added(total, turned(values[j], sign * j * m, count))
            result.append(total)
        return result
    even = short_transform(values[0::2], sign)
    odd = short_transform(values[1::2], sign)
    half = count // 2
    odd = [turned(value, sign * m, count) for m, value in enumerate(odd)]
    minus = [turned(value, 1, 2) for value in odd]
    return [added(e, o) for e, o in zip(even, odd)] + [added(e, o) for e, o in zip(even, minus)]


def dot(left, right):
    return jnp.dot(left, right, preferred_element_type=F32)


def dot_t(left, right):
    return lax.dot_general(left, right, (((1,), (1,)), ((), ())), preferred_element_type=F32)


def times(lr, li, rr, ri):
    return dot(lr, rr) - dot(li, ri), dot(lr, ri) + dot(li, rr)


def times_adjoint(lr, li, rr, ri):
    return dot_t(lr, rr) + dot_t(li, ri), dot_t(li, rr) - dot_t(lr, ri)


def kernel(
    groups, slices, cores,
    gd_hbm, gu_hbm, s_hbm, w_hbm, out_ref,
    fwd_ref, inv_ref, gd, gu, sig, scr, snext, loan, own,
    lbuf, lred, ents, entr, zbuf, qbuf, pbuf, back, rbuf, redp,
    in_sem, z_send, z_recv, l_sem, a_send, a_recv, r_send, r_recv, b_send, b_recv, d_sem,
):
    me = lax.axis_index("energy")
    cut = lax.axis_index("cuts")
    local, _, size, _ = gd.shape
    blocks = lbuf.shape[2]
    extra = (size // SUB - blocks * groups) // cores

    barrier = pltpu.get_barrier_semaphore()

    first = lax.rem(me, 2)
    partner = me + 1 - 2 * first
    last = local - 1

    def greet(k, carry):
        pl.semaphore_signal(
            barrier, inc=1, device_id={"energy": lax.rem(me + k, groups)}, device_id_type=MESH
        )
        return carry

    @pl.when(cut > 0)
    def _():
        for who in (me, partner):
            pl.semaphore_signal(
                barrier, inc=1, device_id={"energy": who, "cuts": cut - 1}, device_id_type=MESH
            )

    @pl.when(cut < slices - 1)
    def _():
        for who in (me, partner):
            pl.semaphore_signal(
                barrier, inc=1, device_id={"energy": who, "cuts": cut + 1}, device_id_type=MESH
            )

    lax.fori_loop(1, groups, greet, 0)

    loads = [
        pltpu.make_async_copy(source, target, in_sem.at[i])
        for i, (source, target) in enumerate(
            [(gd_hbm, gd), (s_hbm, sig), (gu_hbm, gu), (w_hbm, scr)]
        )
    ]
    loads[0].start()
    loads[1].start()

    edges = jnp.where(cut > 0, 1, 0) + jnp.where(cut < slices - 1, 1, 0)
    pl.semaphore_wait(barrier, groups - 1 + 2 * edges)

    def shift(j):
        return pltpu.make_async_remote_copy(
            src_ref=s_hbm.at[j], dst_ref=snext.at[j],
            send_sem=z_send.at[j], recv_sem=z_recv.at[j],
            device_id={"energy": me, "cuts": cut - 1}, device_id_type=MESH,
        )

    def lend():
        return pltpu.make_async_remote_copy(
            src_ref=s_hbm.at[last, 1 - first], dst_ref=loan,
            send_sem=l_sem.at[0], recv_sem=l_sem.at[1],
            device_id={"energy": partner, "cuts": cut}, device_id_type=MESH,
        )

    def shift_mine():
        return pltpu.make_async_remote_copy(
            src_ref=s_hbm.at[last, first], dst_ref=snext.at[last, first],
            send_sem=z_send.at[last], recv_sem=z_recv.at[last],
            device_id={"energy": me, "cuts": cut - 1}, device_id_type=MESH,
        )

    def shift_loan():
        return pltpu.make_async_remote_copy(
            src_ref=loan, dst_ref=snext.at[last, first],
            send_sem=z_send.at[local], recv_sem=z_recv.at[local],
            device_id={"energy": partner, "cuts": cut - 1}, device_id_type=MESH,
        )

    @pl.when(cut > 0)
    def _():
        lend().start()
        for j in range(last):
            shift(j).start()
        lend().wait_recv()

        @pl.when(first == 0)
        def _():
            shift_mine().start()
            shift_loan().start()

        @pl.when(first == 1)
        def _():
            shift_loan().start()
            shift_mine().start()

    for load in loads[2:]:
        load.start()
    fill_tables(fwd_ref, inv_ref, groups, local)
    loads[0].wait()
    loads[1].wait()

    def own_step(j, carry):
        tr, ti = times(gd[j, 0], gd[j, 1], sig[j, 0], sig[j, 1])
        lr, li = times_adjoint(tr.astype(BF16), ti.astype(BF16), gd[j, 0], gd[j, 1])
        own[j, 0] = lr
        own[j, 1] = li
        return carry

    lax.fori_loop(0, local, own_step, 0)
    for load in loads[2:]:
        load.wait()

    def lesser_step(j, carry):
        @pl.when(cut < slices - 1)
        def _():
            @pl.when(j < last)
            def _():
                shift(j).wait_recv()

            @pl.when(j == last)
            def _():
                shift_mine().wait_recv()
                shift_loan().wait_recv()

            tr, ti = times(gu[j, 0], gu[j, 1], snext[j, 0], snext[j, 1])
            lr, li = times_adjoint(tr.astype(BF16), ti.astype(BF16), gu[j, 0], gu[j, 1])
            own[j, 0] += lr
            own[j, 1] += li

        for c in range(2):
            value = own[j, c].astype(BF16).reshape(size // SUB, SUB, size)
            for b in range(blocks):
                for d in range(groups):
                    lbuf[j, d, b, c] = value[b * groups + d]
            for i in range(cores * extra):
                lred[j, i // extra, i % extra, c] = value[blocks * groups + i]

        def send(k, inner):
            to = lax.rem(me + k, groups)
            pltpu.make_async_remote_copy(
                src_ref=lbuf.at[j, to], dst_ref=ents.at[j, me],
                send_sem=a_send.at[j], recv_sem=a_recv.at[j],
                device_id={"energy": to}, device_id_type=MESH,
            ).start()
            return inner

        lax.fori_loop(1, groups, send, 0)

        def send_extra(k, inner):
            to = lax.rem(me + k, groups)
            pltpu.make_async_remote_copy(
                src_ref=lred.at[j, lax.rem(to, cores)], dst_ref=entr.at[j, me],
                send_sem=r_send.at[j], recv_sem=r_recv.at[j],
                device_id={"energy": to}, device_id_type=MESH,
            ).start()
            return inner

        if extra:
            lax.fori_loop(1, groups, send_extra, 0)
            entr[j, me] = lred[j, lax.rem(me, cores)]
        ents[j, me] = lbuf[j, me]
        return carry

    lax.fori_loop(0, local, lesser_step, 0)

    half = 2 * groups * SUB
    slots = [u if 2 * u <= local else local - u for u in range(local)]
    offset = [max(0, 2 * u - 1) for u in range(local // 2 + 1)]

    def spectrum(entries, b):
        for j in range(local):
            x = entries[j, :, b].reshape(half, size)
            zbuf[j] = dot(fwd_ref[j], x)
        step = 2 * SUB
        for at in range(0, half, step):
            for lane in range(0, size, LANES):
                lanes = slice(lane, lane + LANES)
                z = [(zbuf[j, at : at + step, lanes], zbuf[j, half + at : half + at + step, lanes]) for j in range(local)]
                power = [(re * re + im * im, None) for re, im in short_transform(z, -1)]
                for u, (re, im) in enumerate(short_transform(power, 1)[: local // 2 + 1]):
                    qbuf[offset[u], at : at + step, lanes] = re.astype(BF16)
                    if 0 < 2 * u < local:
                        qbuf[offset[u] + 1, at : at + step, lanes] = im.astype(BF16)

    def lags(u, rows):
        slot = slots[u]
        if 0 < 2 * slot < local:
            q = qbuf[offset[slot] : offset[slot] + 2].reshape(2 * half, size)
            return dot(inv_ref[u, rows, :], q)
        return dot(inv_ref[u, rows, :half], qbuf[offset[slot]])

    for j in range(local):
        landed = ents.at[j, pl.ds(0, groups - 1)]
        pltpu.make_async_copy(landed, landed, a_recv.at[j]).wait()

    def block_step(b, carry):
        spectrum(ents, b)
        for u in range(local):
            pbuf[b, u] = lags(u, slice(None)).reshape(groups, 2, SUB, size).astype(BF16)

            def send(k, inner):
                to = lax.rem(me + k, groups)
                pltpu.make_async_remote_copy(
                    src_ref=pbuf.at[b, u, to], dst_ref=back.at[u, b, me],
                    send_sem=b_send.at[b, u], recv_sem=b_recv.at[b, u],
                    device_id={"energy": to}, device_id_type=MESH,
                ).start()
                return inner

            lax.fori_loop(1, groups, send, 0)
            back[u, b, me] = pbuf[b, u, me]
        return carry

    lax.fori_loop(0, blocks, block_step, 0)

    def hand_over():
        return pltpu.make_async_remote_copy(
            src_ref=rbuf, dst_ref=redp.at[first],
            send_sem=d_sem.at[0], recv_sem=d_sem.at[1],
            device_id={"energy": partner}, device_id_type=MESH,
        )

    if extra:
        for j in range(local):
            landed = entr.at[j, pl.ds(0, groups - 1)]
            pltpu.make_async_copy(landed, landed, r_recv.at[j]).wait()

        def extra_step(i, carry):
            spectrum(entr, i)
            step = 2 * SUB
            for u in range(local):
                mine = lags(u, pl.ds(pl.multiple_of(me * step, step), step))
                theirs = lags(u, pl.ds(pl.multiple_of(partner * step, step), step))
                redp[first, u, i] = mine.reshape(2, SUB, size).astype(BF16)
                rbuf[u, i] = theirs.reshape(2, SUB, size).astype(BF16)
            return carry

        lax.fori_loop(0, extra, extra_step, 0)
        hand_over().start()
        hand_over().wait_recv()

    def result_step(u, carry):
        for b in range(blocks):
            landed = back.at[u, b, pl.ds(0, groups - 1)]
            pltpu.make_async_copy(landed, landed, b_recv.at[b, u]).wait()
        polar = []
        for c in range(2):
            value = back[u, :, :, c].reshape(blocks * groups * SUB, size)
            if extra:
                value = jnp.concatenate([value, redp[:, u, :, c].reshape(cores * extra * SUB, size)], axis=0)
            polar.append(value)
        tr, ti = times(scr[u, 0], scr[u, 1], polar[0], polar[1])
        lr, li = times_adjoint(tr.astype(BF16), ti.astype(BF16), scr[u, 0], scr[u, 1])
        out_ref[u, 0] = lr.astype(BF16)
        out_ref[u, 1] = li.astype(BF16)
        return carry

    lax.fori_loop(0, local, result_step, 0)

    @pl.when(cut > 0)
    def _():
        for j in range(last):
            shift(j).wait_send()
        shift_mine().wait_send()
        shift_loan().wait_send()
        lend().wait_send()

    for j in range(local):
        sent = lbuf.at[j, pl.ds(0, groups - 1)]
        pltpu.make_async_copy(sent, sent, a_send.at[j]).wait()
        if extra:
            sent = entr.at[j, pl.ds(0, groups - 1)]
            pltpu.make_async_copy(sent, sent, r_send.at[j]).wait()
        for b in range(blocks):
            sent = pbuf.at[b, j, pl.ds(0, groups - 1)]
            pltpu.make_async_copy(sent, sent, b_send.at[b, j]).wait()
    if extra:
        hand_over().wait_send()


def solution(mesh):
    groups, slices = mesh.shape["energy"], mesh.shape["cuts"]
    cores = 2

    def shards(green_diag, green_upper, sigma_lesser, screening):
        shape = green_diag.shape[1:]
        local, _, size, _ = shape
        shared = size // SHARE
        if (size - shared) % (groups * SUB) or shared % (cores * SUB):
            shared = 0
        blocks = (size - shared) // (groups * SUB)
        extra = shared // (cores * SUB)
        some = max(1, extra)
        half = 2 * groups * SUB
        tile = (2, SUB, size)
        block = pltpu.VMEM(shape, BF16)
        dma = pltpu.SemaphoreType.DMA
        anywhere = pl.BlockSpec(memory_space=pltpu.HBM)
        result = pl.pallas_call(
            functools.partial(kernel, groups, slices, cores),
            out_shape=jax.ShapeDtypeStruct(shape, BF16),
            in_specs=[anywhere] * 4,
            out_specs=pl.BlockSpec(memory_space=pltpu.VMEM),
            scratch_shapes=[
                pltpu.VMEM((local, 2 * half, half), BF16),
                pltpu.VMEM((local, half, 2 * half), BF16),
                block, block, block, block, block,
                pltpu.VMEM(shape[2:], BF16),
                pltpu.VMEM(shape, F32),
                pltpu.VMEM((local, groups, blocks) + tile, BF16),
                pltpu.VMEM((local, cores, some) + tile, BF16),
                pltpu.VMEM((local, groups, blocks) + tile, BF16),
                pltpu.VMEM((local, groups, some) + tile, BF16),
                pltpu.VMEM((local, 2 * half, size), F32),
                pltpu.VMEM((local, half, size), BF16),
                pltpu.VMEM((blocks, local, groups) + tile, BF16),
                pltpu.VMEM((local, blocks, groups) + tile, BF16),
                pltpu.VMEM((local, some) + tile, BF16),
                pltpu.VMEM((cores, local, some) + tile, BF16),
                dma((4,)),
                dma((local + 1,)), dma((local + 1,)), dma((2,)),
                dma((local,)), dma((local,)), dma((local,)), dma((local,)),
                dma((blocks, local)), dma((blocks, local)), dma((2,)),
            ],
            compiler_params=pltpu.CompilerParams(
                collective_id=0, has_side_effects=True, vmem_limit_bytes=54525952
            ),
        )(
            green_diag[0], green_upper[0], sigma_lesser[0], screening[0]
        )
        return result[None]

    spec = P("cuts", "energy", None, None, None)
    return jax.shard_map(
        shards, mesh=mesh, in_specs=(spec,) * 4, out_specs=spec, check_vma=False
    )
```

```python
import functools
import math

import jax
import jax.numpy as jnp
from jax import lax
from jax.experimental import pallas as pl
from jax.experimental.pallas import tpu as pltpu
from jax.sharding import PartitionSpec as P

LANES = 128
SUB = 8
SHARE = 4
MESH = pl.DeviceIdType.MESH
F32 = jnp.float32
BF16 = jnp.bfloat16


def fill_tables(fwd_ref, inv_ref, groups, local):
    width = 2 * groups
    period = width * local

    def index(shape, axis, unit, count):
        return lax.rem(lax.div(lax.broadcasted_iota(jnp.int32, shape, axis), unit), count)

    def table(shape, phase, quarters, scale):
        turn = lax.rem(phase + quarters * (period // 4), period)
        value = jnp.cos(turn.astype(F32) * (2.0 * math.pi / period)) * scale
        same = index(shape, 0, 1, SUB) == index(shape, 1, 1, SUB)
        return jnp.where(same, value, 0.0).astype(BF16)

    for j in range(local):
        shape = fwd_ref.shape[1:]
        point = index(shape, 0, SUB, width)
        turn = index(shape, 0, SUB * width, 2) - index(shape, 1, SUB, 2) + 4
        energy = index(shape, 1, 2 * SUB, groups) * local + j
        fwd_ref[j] = table(shape, lax.rem(point * energy, period), turn, 1.0)

        shape = inv_ref.shape[1:]
        component = index(shape, 0, SUB, 2)
        part = index(shape, 1, SUB * width, 2)
        lag = index(shape, 0, 2 * SUB, groups) * local + j
        other = 1 - component if 2 * j <= local else 3 - component
        turn = jnp.where(part == 0, 3 * component, other)
        point = index(shape, 1, SUB, width)
        inv_ref[j] = table(shape, lax.rem(point * lag, period), turn, 2.0 / period / period)


def negated(x):
    return None if x is None else -x


def scaled(x, factor):
    return None if x is None else x * factor


def turned(value, numerator, denominator):
    re, im = value
    angle = numerator % denominator
    if angle == 0:
        return re, im
    if 2 * angle == denominator:
        return negated(re), negated(im)
    if 4 * angle == denominator:
        return negated(im), re
    if 4 * angle == 3 * denominator:
        return im, negated(re)
    c = math.cos(2.0 * math.pi * angle / denominator)
    s = math.sin(2.0 * math.pi * angle / denominator)
    return added((scaled(re, c), scaled(re, s)), (scaled(im, -s), scaled(im, c)))


def added(left, right):
    def one(x, y):
        return y if x is None else x if y is None else x + y

    return one(left[0], right[0]), one(left[1], right[1])


def short_transform(values, sign):
    count = len(values)
    if count == 1:
        return values
    if count % 2:
        result = []
        for m in range(count):
            total = values[0]
            for j in range(1, count):
                total = added(total, turned(values[j], sign * j * m, count))
            result.append(total)
        return result
    even = short_transform(values[0::2], sign)
    odd = short_transform(values[1::2], sign)
    half = count // 2
    odd = [turned(value, sign * m, count) for m, value in enumerate(odd)]
    minus = [turned(value, 1, 2) for value in odd]
    return [added(e, o) for e, o in zip(even, odd)] + [added(e, o) for e, o in zip(even, minus)]


def dot(left, right):
    return jnp.dot(left, right, preferred_element_type=F32)


def dot_t(left, right):
    return lax.dot_general(left, right, (((1,), (1,)), ((), ())), preferred_element_type=F32)


def times(lr, li, rr, ri):
    return dot(lr, rr) - dot(li, ri), dot(lr, ri) + dot(li, rr)


def times_adjoint(lr, li, rr, ri):
    return dot_t(lr, rr) + dot_t(li, ri), dot_t(li, rr) - dot_t(lr, ri)


def kernel(
    groups, slices, cores,
    gd_hbm, gu_hbm, s_hbm, w_hbm, out_ref,
    fwd_ref, inv_ref, gd, gu, sig, scr, snext, loan, own,
    lbuf, lred, ents, entr, zbuf, qbuf, pbuf, back, rbuf, redp,
    ready, go, in_sem, z_send, z_recv, l_send, l_recv, a_send, a_recv, r_send, r_recv, b_send, b_recv, d_sem,
):
    me = lax.axis_index("energy")
    cut = lax.axis_index("cuts")
    local, _, size, _ = gd.shape
    blocks = lbuf.shape[2]
    extra = (size // SUB - blocks * groups) // cores

    barrier = pltpu.get_barrier_semaphore()

    first = lax.rem(me, 2)
    partner = me + 1 - 2 * first
    last = local - 1

    @pl.when(cut < slices - 1)
    def _():
        for who in (me, partner):
            pl.semaphore_signal(
                barrier, inc=1, device_id={"energy": who, "cuts": cut + 1}, device_id_type=MESH
            )

    pl.semaphore_signal(barrier, inc=1, device_id={"energy": partner}, device_id_type=MESH)

    def to_others(semaphore):
        def greet(k, carry):
            pl.semaphore_signal(semaphore, inc=1, device_id={"energy": k}, device_id_type=MESH)
            return carry

        lax.fori_loop(1, groups, greet, 0)

    @pl.when(me == 0)
    def _():
        to_others(barrier)

    loads = [
        pltpu.make_async_copy(source, target, in_sem.at[i])
        for i, (source, target) in enumerate(
            [(gd_hbm, gd), (s_hbm, sig), (gu_hbm, gu), (w_hbm, scr)]
        )
    ]
    pl.semaphore_wait(
        barrier, 1 + jnp.where(me > 0, 1, 0) + 2 * jnp.where(cut > 0, 1, 0)
    )

    def lend(j):
        return pltpu.make_async_remote_copy(
            src_ref=s_hbm.at[j, 1 - first], dst_ref=loan.at[j],
            send_sem=l_send.at[j], recv_sem=l_recv.at[j],
            device_id={"energy": partner, "cuts": cut}, device_id_type=MESH,
        )

    def shift_mine(j):
        return pltpu.make_async_remote_copy(
            src_ref=s_hbm.at[j, first], dst_ref=snext.at[j, first],
            send_sem=z_send.at[0, j], recv_sem=z_recv.at[0, j],
            device_id={"energy": me, "cuts": cut - 1}, device_id_type=MESH,
        )

    def shift_loan(j):
        return pltpu.make_async_remote_copy(
            src_ref=loan.at[j], dst_ref=snext.at[j, first],
            send_sem=z_send.at[1, j], recv_sem=z_recv.at[1, j],
            device_id={"energy": partner, "cuts": cut - 1}, device_id_type=MESH,
        )

    @pl.when(cut > 0)
    def _():
        for j in range(local):
            lend(j).start()

        @pl.when(first == 0)
        def _():
            for j in range(local):
                shift_mine(j).start()
                lend(j).wait_recv()
                shift_loan(j).start()

        @pl.when(first == 1)
        def _():
            for j in range(local):
                lend(j).wait_recv()
                shift_loan(j).start()
                shift_mine(j).start()

    for load in loads:
        load.start()

    @pl.when(me > 0)
    def _():
        pl.semaphore_signal(ready, inc=1, device_id={"energy": 0}, device_id_type=MESH)

    @pl.when(me == 0)
    def _():
        pl.semaphore_wait(ready, groups - 1)
        to_others(go)

    for load in loads:
        load.wait()

    half = 2 * groups * SUB

    def forward(entries, base, j, b):
        zbuf[base + b, j] = dot(fwd_ref[j], entries[j, :, b].reshape(half, size))

    def arrived(entries, semaphore, j):
        landed = entries.at[j, pl.ds(0, groups - 1)]
        pltpu.make_async_copy(landed, landed, semaphore.at[j]).wait()

    def each(count, body):
        lax.fori_loop(0, count, lambda b, carry: (body(b), carry)[1], 0)

    def lesser_step(j, carry):
        tr, ti = times(gd[j, 0], gd[j, 1], sig[j, 0], sig[j, 1])
        lr, li = times_adjoint(tr.astype(BF16), ti.astype(BF16), gd[j, 0], gd[j, 1])
        own[0] = lr
        own[1] = li

        @pl.when(j == min(1, last))
        def _():
            fill_tables(fwd_ref, inv_ref, groups, local)

        @pl.when(cut < slices - 1)
        def _():
            shift_mine(j).wait_recv()
            shift_loan(j).wait_recv()
            tr, ti = times(gu[j, 0], gu[j, 1], snext[j, 0], snext[j, 1])
            lr, li = times_adjoint(tr.astype(BF16), ti.astype(BF16), gu[j, 0], gu[j, 1])
            own[0] += lr
            own[1] += li

        for c in range(2):
            value = own[c].astype(BF16).reshape(size // SUB, SUB, size)
            for b in range(blocks):
                for d in range(groups):
                    lbuf[j, d, b, c] = value[b * groups + d]
            for i in range(cores * extra):
                lred[j, i // extra, i % extra, c] = value[blocks * groups + i]

        @pl.when((j == 0) & (me > 0))
        def _():
            pl.semaphore_wait(go, 1)

        def send(k, inner):
            to = lax.rem(me + k, groups)
            pltpu.make_async_remote_copy(
                src_ref=lbuf.at[j, to], dst_ref=ents.at[j, me],
                send_sem=a_send.at[j], recv_sem=a_recv.at[j],
                device_id={"energy": to}, device_id_type=MESH,
            ).start()
            return inner

        lax.fori_loop(1, groups, send, 0)

        def send_extra(k, inner):
            to = lax.rem(me + k, groups)
            pltpu.make_async_remote_copy(
                src_ref=lred.at[j, lax.rem(to, cores)], dst_ref=entr.at[j, me],
                send_sem=r_send.at[j], recv_sem=r_recv.at[j],
                device_id={"energy": to}, device_id_type=MESH,
            ).start()
            return inner

        if extra:
            lax.fori_loop(1, groups, send_extra, 0)
            entr[j, me] = lred[j, lax.rem(me, cores)]
        ents[j, me] = lbuf[j, me]

        @pl.when(j > 0)
        def _():
            arrived(ents, a_recv, j - 1)
            each(blocks, lambda b: forward(ents, 0, j - 1, b))
            if extra:
                arrived(entr, r_recv, j - 1)
                each(extra, lambda b: forward(entr, blocks, j - 1, b))

        return carry

    lax.fori_loop(0, local, lesser_step, 0)

    slots = [u if 2 * u <= local else local - u for u in range(local)]
    offset = [max(0, 2 * u - 1) for u in range(local // 2 + 1)]

    def spectrum(entries, base, b):
        forward(entries, base, last, b)
        step = 2 * SUB
        for at in range(0, half, step):
            for lane in range(0, size, LANES):
                lanes = slice(lane, lane + LANES)
                z = [
                    (zbuf[base + b, j, at : at + step, lanes], zbuf[base + b, j, half + at : half + at + step, lanes])
                    for j in range(local)
                ]
                power = [(re * re + im * im, None) for re, im in short_transform(z, -1)]
                for u, (re, im) in enumerate(short_transform(power, 1)[: local // 2 + 1]):
                    qbuf[offset[u], at : at + step, lanes] = re.astype(BF16)
                    if 0 < 2 * u < local:
                        qbuf[offset[u] + 1, at : at + step, lanes] = im.astype(BF16)

    def lags(u, rows):
        slot = slots[u]
        if 0 < 2 * slot < local:
            q = qbuf[offset[slot] : offset[slot] + 2].reshape(2 * half, size)
            return dot(inv_ref[u, rows, :], q)
        return dot(inv_ref[u, rows, :half], qbuf[offset[slot]])

    arrived(ents, a_recv, last)

    def block_step(b, carry):
        spectrum(ents, 0, b)
        for u in range(local):
            pbuf[b, u] = lags(u, slice(None)).reshape(groups, 2, SUB, size).astype(BF16)

            def send(k, inner):
                to = lax.rem(me + k, groups)
                pltpu.make_async_remote_copy(
                    src_ref=pbuf.at[b, u, to], dst_ref=back.at[u, b, me],
                    send_sem=b_send.at[b, u], recv_sem=b_recv.at[b, u],
                    device_id={"energy": to}, device_id_type=MESH,
                ).start()
                return inner

            lax.fori_loop(1, groups, send, 0)
            back[u, b, me] = pbuf[b, u, me]
        return carry

    lax.fori_loop(0, blocks, block_step, 0)

    def hand_over():
        return pltpu.make_async_remote_copy(
            src_ref=rbuf, dst_ref=redp.at[first],
            send_sem=d_sem.at[0], recv_sem=d_sem.at[1],
            device_id={"energy": partner}, device_id_type=MESH,
        )

    if extra:
        arrived(entr, r_recv, last)

        def extra_step(i, carry):
            spectrum(entr, blocks, i)
            step = 2 * SUB
            for u in range(local):
                mine = lags(u, pl.ds(pl.multiple_of(me * step, step), step))
                theirs = lags(u, pl.ds(pl.multiple_of(partner * step, step), step))
                redp[first, u, i] = mine.reshape(2, SUB, size).astype(BF16)
                rbuf[u, i] = theirs.reshape(2, SUB, size).astype(BF16)
            return carry

        lax.fori_loop(0, extra, extra_step, 0)
        hand_over().start()
        hand_over().wait_recv()

    def result_step(u, carry):
        for b in range(blocks):
            landed = back.at[u, b, pl.ds(0, groups - 1)]
            pltpu.make_async_copy(landed, landed, b_recv.at[b, u]).wait()
        polar = []
        for c in range(2):
            value = back[u, :, :, c].reshape(blocks * groups * SUB, size)
            if extra:
                value = jnp.concatenate([value, redp[:, u, :, c].reshape(cores * extra * SUB, size)], axis=0)
            polar.append(value)
        tr, ti = times(scr[u, 0], scr[u, 1], polar[0], polar[1])
        lr, li = times_adjoint(tr.astype(BF16), ti.astype(BF16), scr[u, 0], scr[u, 1])
        out_ref[u, 0] = lr.astype(BF16)
        out_ref[u, 1] = li.astype(BF16)
        return carry

    lax.fori_loop(0, local, result_step, 0)

    @pl.when(cut > 0)
    def _():
        for j in range(local):
            shift_mine(j).wait_send()
            shift_loan(j).wait_send()
            lend(j).wait_send()

    for j in range(local):
        sent = lbuf.at[j, pl.ds(0, groups - 1)]
        pltpu.make_async_copy(sent, sent, a_send.at[j]).wait()
        if extra:
            sent = entr.at[j, pl.ds(0, groups - 1)]
            pltpu.make_async_copy(sent, sent, r_send.at[j]).wait()
        for b in range(blocks):
            sent = pbuf.at[b, j, pl.ds(0, groups - 1)]
            pltpu.make_async_copy(sent, sent, b_send.at[b, j]).wait()
    if extra:
        hand_over().wait_send()


def solution(mesh):
    groups, slices = mesh.shape["energy"], mesh.shape["cuts"]
    cores = 2

    def shards(green_diag, green_upper, sigma_lesser, screening):
        shape = green_diag.shape[1:]
        local, _, size, _ = shape
        shared = size // SHARE
        if (size - shared) % (groups * SUB) or shared % (cores * SUB):
            shared = 0
        blocks = (size - shared) // (groups * SUB)
        extra = shared // (cores * SUB)
        some = max(1, extra)
        half = 2 * groups * SUB
        tile = (2, SUB, size)
        block = pltpu.VMEM(shape, BF16)
        dma = pltpu.SemaphoreType.DMA
        anywhere = pl.BlockSpec(memory_space=pltpu.HBM)
        result = pl.pallas_call(
            functools.partial(kernel, groups, slices, cores),
            out_shape=jax.ShapeDtypeStruct(shape, BF16),
            in_specs=[anywhere] * 4,
            out_specs=pl.BlockSpec(memory_space=pltpu.VMEM),
            scratch_shapes=[
                pltpu.VMEM((local, 2 * half, half), BF16),
                pltpu.VMEM((local, half, 2 * half), BF16),
                block, block, block, block, block,
                pltpu.VMEM((local,) + shape[2:], BF16),
                pltpu.VMEM(shape[1:], F32),
                pltpu.VMEM((local, groups, blocks) + tile, BF16),
                pltpu.VMEM((local, cores, some) + tile, BF16),
                pltpu.VMEM((local, groups, blocks) + tile, BF16),
                pltpu.VMEM((local, groups, some) + tile, BF16),
                pltpu.VMEM((blocks + extra, local, 2 * half, size), F32),
                pltpu.VMEM((local, half, size), BF16),
                pltpu.VMEM((blocks, local, groups) + tile, BF16),
                pltpu.VMEM((local, blocks, groups) + tile, BF16),
                pltpu.VMEM((local, some) + tile, BF16),
                pltpu.VMEM((cores, local, some) + tile, BF16),
                pltpu.SemaphoreType.REGULAR, pltpu.SemaphoreType.REGULAR,
                dma((4,)),
                dma((2, local)), dma((2, local)), dma((local,)), dma((local,)),
                dma((local,)), dma((local,)), dma((local,)), dma((local,)),
                dma((blocks, local)), dma((blocks, local)), dma((2,)),
            ],
            compiler_params=pltpu.CompilerParams(
                collective_id=0, has_side_effects=True, vmem_limit_bytes=54525952
            ),
        )(
            green_diag[0], green_upper[0], sigma_lesser[0], screening[0]
        )
        return result[None]

    spec = P("cuts", "energy", None, None, None)
    return jax.shard_map(
        shards, mesh=mesh, in_specs=(spec,) * 4, out_specs=spec, check_vma=False
    )
```

```python
import functools
import math

import jax
import jax.numpy as jnp
from jax import lax
from jax.experimental import pallas as pl
from jax.experimental.pallas import tpu as pltpu
from jax.sharding import PartitionSpec as P

LANES = 128
SUB = 8
SHARE = 4
MESH = pl.DeviceIdType.MESH
F32 = jnp.float32
BF16 = jnp.bfloat16


def fill_tables(fwd_ref, inv_ref, groups, local):
    width = 2 * groups
    period = width * local

    def index(shape, axis, unit, count):
        return lax.rem(lax.div(lax.broadcasted_iota(jnp.int32, shape, axis), unit), count)

    def table(shape, phase, quarters, scale):
        turn = lax.rem(phase + quarters * (period // 4), period)
        value = jnp.cos(turn.astype(F32) * (2.0 * math.pi / period)) * scale
        same = index(shape, 0, 1, SUB) == index(shape, 1, 1, SUB)
        return jnp.where(same, value, 0.0).astype(BF16)

    for j in range(local):
        shape = fwd_ref.shape[1:]
        point = index(shape, 0, SUB, width)
        turn = index(shape, 0, SUB * width, 2) - index(shape, 1, SUB, 2) + 4
        energy = index(shape, 1, 2 * SUB, groups) * local + j
        fwd_ref[j] = table(shape, lax.rem(point * energy, period), turn, 1.0)

        shape = inv_ref.shape[1:]
        component = index(shape, 0, SUB, 2)
        part = index(shape, 1, SUB * width, 2)
        lag = index(shape, 0, 2 * SUB, groups) * local + j
        other = 1 - component if 2 * j <= local else 3 - component
        turn = jnp.where(part == 0, 3 * component, other)
        point = index(shape, 1, SUB, width)
        inv_ref[j] = table(shape, lax.rem(point * lag, period), turn, 2.0 / period / period)


def negated(x):
    return None if x is None else -x


def scaled(x, factor):
    return None if x is None else x * factor


def turned(value, numerator, denominator):
    re, im = value
    angle = numerator % denominator
    if angle == 0:
        return re, im
    if 2 * angle == denominator:
        return negated(re), negated(im)
    if 4 * angle == denominator:
        return negated(im), re
    if 4 * angle == 3 * denominator:
        return im, negated(re)
    c = math.cos(2.0 * math.pi * angle / denominator)
    s = math.sin(2.0 * math.pi * angle / denominator)
    return added((scaled(re, c), scaled(re, s)), (scaled(im, -s), scaled(im, c)))


def added(left, right):
    def one(x, y):
        return y if x is None else x if y is None else x + y

    return one(left[0], right[0]), one(left[1], right[1])


def short_transform(values, sign):
    count = len(values)
    if count == 1:
        return values
    if count % 2:
        result = []
        for m in range(count):
            total = values[0]
            for j in range(1, count):
                total = added(total, turned(values[j], sign * j * m, count))
            result.append(total)
        return result
    even = short_transform(values[0::2], sign)
    odd = short_transform(values[1::2], sign)
    half = count // 2
    odd = [turned(value, sign * m, count) for m, value in enumerate(odd)]
    minus = [turned(value, 1, 2) for value in odd]
    return [added(e, o) for e, o in zip(even, odd)] + [added(e, o) for e, o in zip(even, minus)]


def dot(left, right):
    return jnp.dot(left, right, preferred_element_type=F32)


def dot_t(left, right):
    return lax.dot_general(left, right, (((1,), (1,)), ((), ())), preferred_element_type=F32)


def beside(left, right):
    return jnp.concatenate([left, right], axis=1)


def above(top, bottom):
    return jnp.concatenate([top, bottom], axis=0)


def sandwich(re, im, negative, middle_re, middle_im):
    middle = above(middle_re, middle_im)
    tr = dot(beside(re, negative), middle).astype(BF16)
    ti = dot(beside(im, re), middle).astype(BF16)
    left = beside(tr, ti)
    return dot_t(left, beside(re, im)), dot_t(left, beside(negative, re))


def kernel(
    groups, slices, cores,
    gd_hbm, gu_hbm, s_hbm, w_hbm, out_ref,
    fwd_ref, inv_ref, gd, gu, sig, scr, snext, loan, own, minus, wminus,
    lbuf, lred, ents, entr, zbuf, qbuf, pbuf, back, rbuf, redp,
    ready, go, in_sem, z_send, z_recv, l_send, l_recv, a_send, a_recv, r_send, r_recv, b_send, b_recv, d_sem,
):
    me = lax.axis_index("energy")
    cut = lax.axis_index("cuts")
    local, _, size, _ = gd.shape
    blocks = lbuf.shape[1]
    extra = (size // SUB - blocks * groups) // cores

    barrier = pltpu.get_barrier_semaphore()

    first = lax.rem(me, 2)
    partner = me + 1 - 2 * first
    last = local - 1

    @pl.when(cut < slices - 1)
    def _():
        for who in (me, partner):
            pl.semaphore_signal(
                barrier, inc=1, device_id={"energy": who, "cuts": cut + 1}, device_id_type=MESH
            )

    pl.semaphore_signal(barrier, inc=1, device_id={"energy": partner}, device_id_type=MESH)

    def to_others(semaphore):
        def greet(k, carry):
            pl.semaphore_signal(semaphore, inc=1, device_id={"energy": k}, device_id_type=MESH)
            return carry

        lax.fori_loop(1, groups, greet, 0)

    @pl.when(me == 0)
    def _():
        to_others(barrier)

    loads = [
        pltpu.make_async_copy(source, target, in_sem.at[i])
        for i, (source, target) in enumerate(
            [(gd_hbm, gd), (s_hbm, sig), (gu_hbm, gu), (w_hbm, scr)]
        )
    ]
    pl.semaphore_wait(
        barrier, 1 + jnp.where(me > 0, 1, 0) + 2 * jnp.where(cut > 0, 1, 0)
    )

    def lend(j):
        return pltpu.make_async_remote_copy(
            src_ref=s_hbm.at[j, 1 - first], dst_ref=loan.at[j],
            send_sem=l_send.at[j], recv_sem=l_recv.at[j],
            device_id={"energy": partner, "cuts": cut}, device_id_type=MESH,
        )

    def shift_mine(j):
        return pltpu.make_async_remote_copy(
            src_ref=s_hbm.at[j, first], dst_ref=snext.at[j, first],
            send_sem=z_send.at[0, j], recv_sem=z_recv.at[0, j],
            device_id={"energy": me, "cuts": cut - 1}, device_id_type=MESH,
        )

    def shift_loan(j):
        return pltpu.make_async_remote_copy(
            src_ref=loan.at[j], dst_ref=snext.at[j, first],
            send_sem=z_send.at[1, j], recv_sem=z_recv.at[1, j],
            device_id={"energy": partner, "cuts": cut - 1}, device_id_type=MESH,
        )

    @pl.when(cut > 0)
    def _():
        for j in range(local):
            lend(j).start()

        @pl.when(first == 0)
        def _():
            for j in range(local):
                shift_mine(j).start()
                lend(j).wait_recv()
                shift_loan(j).start()

        @pl.when(first == 1)
        def _():
            for j in range(local):
                lend(j).wait_recv()
                shift_loan(j).start()
                shift_mine(j).start()

    for load in loads:
        load.start()

    @pl.when(me > 0)
    def _():
        pl.semaphore_signal(ready, inc=1, device_id={"energy": 0}, device_id_type=MESH)

    @pl.when(me == 0)
    def _():
        pl.semaphore_wait(ready, groups - 1)
        to_others(go)

    for load in loads:
        load.wait()

    half = 2 * groups * SUB

    def forward(at, j, entries):
        zbuf[at, j] = dot(fwd_ref[j], entries.reshape(half, size))

    def forward_block(j, b):
        wait_for(ents.at[j, b], a_recv.at[j, b])
        forward(b, j, ents[j, b])

    def wait_for(some, semaphore):
        landed = some.at[pl.ds(0, groups - 1)]
        pltpu.make_async_copy(landed, landed, semaphore).wait()

    def each(count, body):
        lax.fori_loop(0, count, lambda b, carry: (body(b), carry)[1], 0)

    def lesser_step(j, carry):
        own[0], own[1] = sandwich(gd[j, 0], gd[j, 1], -gd[j, 1], sig[j, 0], sig[j, 1])
        minus[...] = -gu[j, 1]
        wminus[j] = -scr[j, 1]

        @pl.when(j == min(1, last))
        def _():
            fill_tables(fwd_ref, inv_ref, groups, local)

        @pl.when(cut < slices - 1)
        def _():
            shift_mine(j).wait_recv()
            shift_loan(j).wait_recv()
            re, im = sandwich(gu[j, 0], gu[j, 1], minus[...], snext[j, 0], snext[j, 1])
            own[0] += re
            own[1] += im

        for c in range(2):
            value = own[c].astype(BF16).reshape(size // SUB, SUB, size)
            for b in range(blocks):
                lbuf[j, b, :, c] = value[b * groups : (b + 1) * groups]
            for i in range(cores * extra):
                lred[j, i // extra, i % extra, c] = value[blocks * groups + i]

        @pl.when((j == 0) & (me > 0))
        def _():
            pl.semaphore_wait(go, 1)

        def spread(b):
            def send(k, inner):
                to = lax.rem(me + k, groups)
                pltpu.make_async_remote_copy(
                    src_ref=lbuf.at[j, b, to], dst_ref=ents.at[j, b, me],
                    send_sem=a_send.at[j, b], recv_sem=a_recv.at[j, b],
                    device_id={"energy": to}, device_id_type=MESH,
                ).start()
                return inner

            lax.fori_loop(1, groups, send, 0)
            ents[j, b, me] = lbuf[j, b, me]

        each(blocks, spread)

        def send_extra(k, inner):
            to = lax.rem(me + k, groups)
            pltpu.make_async_remote_copy(
                src_ref=lred.at[j, lax.rem(to, cores)], dst_ref=entr.at[j, me],
                send_sem=r_send.at[j], recv_sem=r_recv.at[j],
                device_id={"energy": to}, device_id_type=MESH,
            ).start()
            return inner

        if extra:
            lax.fori_loop(1, groups, send_extra, 0)
            entr[j, me] = lred[j, lax.rem(me, cores)]
        @pl.when(j > 0)
        def _():
            each(blocks, lambda b: forward_block(j - 1, b))
            if extra:
                wait_for(entr.at[j - 1], r_recv.at[j - 1])
                each(extra, lambda i: forward(blocks + i, j - 1, entr[j - 1, :, i]))

        return carry

    lax.fori_loop(0, local, lesser_step, 0)

    slots = [u if 2 * u <= local else local - u for u in range(local)]
    offset = [max(0, 2 * u - 1) for u in range(local // 2 + 1)]

    def spectrum(block):
        step = 2 * SUB
        for at in range(0, half, step):
            for lane in range(0, size, LANES):
                lanes = slice(lane, lane + LANES)
                z = [
                    (zbuf[block, j, at : at + step, lanes], zbuf[block, j, half + at : half + at + step, lanes])
                    for j in range(local)
                ]
                power = [(re * re + im * im, None) for re, im in short_transform(z, -1)]
                for u, (re, im) in enumerate(short_transform(power, 1)[: local // 2 + 1]):
                    qbuf[offset[u], at : at + step, lanes] = re.astype(BF16)
                    if 0 < 2 * u < local:
                        qbuf[offset[u] + 1, at : at + step, lanes] = im.astype(BF16)

    def lags(u, rows):
        slot = slots[u]
        if 0 < 2 * slot < local:
            q = qbuf[offset[slot] : offset[slot] + 2].reshape(2 * half, size)
            return dot(inv_ref[u, rows, :], q)
        return dot(inv_ref[u, rows, :half], qbuf[offset[slot]])

    def block_step(b, carry):
        forward_block(last, b)
        spectrum(b)
        for u in range(local):
            pbuf[b, u] = lags(u, slice(None)).reshape(groups, 2, SUB, size).astype(BF16)

            def send(k, inner):
                to = lax.rem(me + k, groups)
                pltpu.make_async_remote_copy(
                    src_ref=pbuf.at[b, u, to], dst_ref=back.at[u, b, me],
                    send_sem=b_send.at[b, u], recv_sem=b_recv.at[b, u],
                    device_id={"energy": to}, device_id_type=MESH,
                ).start()
                return inner

            lax.fori_loop(1, groups, send, 0)
            back[u, b, me] = pbuf[b, u, me]
        return carry

    lax.fori_loop(0, blocks, block_step, 0)

    def hand_over():
        return pltpu.make_async_remote_copy(
            src_ref=rbuf, dst_ref=redp.at[first],
            send_sem=d_sem.at[0], recv_sem=d_sem.at[1],
            device_id={"energy": partner}, device_id_type=MESH,
        )

    if extra:
        wait_for(entr.at[last], r_recv.at[last])

        def extra_step(i, carry):
            forward(blocks + i, last, entr[last, :, i])
            spectrum(blocks + i)
            step = 2 * SUB
            for u in range(local):
                mine = lags(u, pl.ds(pl.multiple_of(me * step, step), step))
                theirs = lags(u, pl.ds(pl.multiple_of(partner * step, step), step))
                redp[first, u, i] = mine.reshape(2, SUB, size).astype(BF16)
                rbuf[u, i] = theirs.reshape(2, SUB, size).astype(BF16)
            return carry

        lax.fori_loop(0, extra, extra_step, 0)
        hand_over().start()
        hand_over().wait_recv()

    def result_step(u, carry):
        for b in range(blocks):
            wait_for(back.at[u, b], b_recv.at[b, u])
        polar = []
        for c in range(2):
            value = back[u, :, :, c].reshape(blocks * groups * SUB, size)
            if extra:
                value = jnp.concatenate([value, redp[:, u, :, c].reshape(cores * extra * SUB, size)], axis=0)
            polar.append(value)
        re, im = sandwich(scr[u, 0], scr[u, 1], wminus[u], polar[0], polar[1])
        out_ref[u, 0] = re.astype(BF16)
        out_ref[u, 1] = im.astype(BF16)
        return carry

    lax.fori_loop(0, local, result_step, 0)

    @pl.when(cut > 0)
    def _():
        for j in range(local):
            shift_mine(j).wait_send()
            shift_loan(j).wait_send()
            lend(j).wait_send()

    for j in range(local):
        if extra:
            wait_for(entr.at[j], r_send.at[j])
        for b in range(blocks):
            wait_for(lbuf.at[j, b], a_send.at[j, b])
            wait_for(pbuf.at[b, j], b_send.at[b, j])
    if extra:
        hand_over().wait_send()


def solution(mesh):
    groups, slices = mesh.shape["energy"], mesh.shape["cuts"]
    cores = 2

    def shards(green_diag, green_upper, sigma_lesser, screening):
        shape = green_diag.shape[1:]
        local, _, size, _ = shape
        shared = size // SHARE
        if (size - shared) % (groups * SUB) or shared % (cores * SUB):
            shared = 0
        blocks = (size - shared) // (groups * SUB)
        extra = shared // (cores * SUB)
        some = max(1, extra)
        half = 2 * groups * SUB
        tile = (2, SUB, size)
        block = pltpu.VMEM(shape, BF16)
        dma = pltpu.SemaphoreType.DMA
        anywhere = pl.BlockSpec(memory_space=pltpu.HBM)
        result = pl.pallas_call(
            functools.partial(kernel, groups, slices, cores),
            out_shape=jax.ShapeDtypeStruct(shape, BF16),
            in_specs=[anywhere] * 4,
            out_specs=pl.BlockSpec(memory_space=pltpu.VMEM),
            scratch_shapes=[
                pltpu.VMEM((local, 2 * half, half), BF16),
                pltpu.VMEM((local, half, 2 * half), BF16),
                block, block, block, block, block,
                pltpu.VMEM((local,) + shape[2:], BF16),
                pltpu.VMEM(shape[1:], F32),
                pltpu.VMEM(shape[2:], BF16),
                pltpu.VMEM((local,) + shape[2:], BF16),
                pltpu.VMEM((local, blocks, groups) + tile, BF16),
                pltpu.VMEM((local, cores, some) + tile, BF16),
                pltpu.VMEM((local, blocks, groups) + tile, BF16),
                pltpu.VMEM((local, groups, some) + tile, BF16),
                pltpu.VMEM((blocks + extra, local, 2 * half, size), F32),
                pltpu.VMEM((local, half, size), BF16),
                pltpu.VMEM((blocks, local, groups) + tile, BF16),
                pltpu.VMEM((local, blocks, groups) + tile, BF16),
                pltpu.VMEM((local, some) + tile, BF16),
                pltpu.VMEM((cores, local, some) + tile, BF16),
                pltpu.SemaphoreType.REGULAR, pltpu.SemaphoreType.REGULAR,
                dma((4,)),
                dma((2, local)), dma((2, local)), dma((local,)), dma((local,)),
                dma((local, blocks)), dma((local, blocks)), dma((local,)), dma((local,)),
                dma((blocks, local)), dma((blocks, local)), dma((2,)),
            ],
            compiler_params=pltpu.CompilerParams(
                collective_id=0, has_side_effects=True, vmem_limit_bytes=54525952
            ),
        )(
            green_diag[0], green_upper[0], sigma_lesser[0], screening[0]
        )
        return result[None]

    spec = P("cuts", "energy", None, None, None)
    return jax.shard_map(
        shards, mesh=mesh, in_specs=(spec,) * 4, out_specs=spec, check_vma=False
    )
```

```python
import functools
import math

import jax
import jax.numpy as jnp
from jax import lax
from jax.experimental import pallas as pl
from jax.experimental.pallas import tpu as pltpu
from jax.sharding import PartitionSpec as P

LANES = 128
SUB = 8
SHARE = 4
MESH = pl.DeviceIdType.MESH
F32 = jnp.float32
BF16 = jnp.bfloat16


def fill_tables(fwd_ref, inv_ref, groups, local):
    width = 2 * groups
    period = width * local

    def index(shape, axis, unit, count):
        return lax.rem(lax.div(lax.broadcasted_iota(jnp.int32, shape, axis), unit), count)

    def table(shape, phase, quarters, scale):
        turn = lax.rem(phase + quarters * (period // 4), period)
        value = jnp.cos(turn.astype(F32) * (2.0 * math.pi / period)) * scale
        same = index(shape, 0, 1, SUB) == index(shape, 1, 1, SUB)
        return jnp.where(same, value, 0.0).astype(BF16)

    for j in range(local):
        shape = fwd_ref.shape[1:]
        point = index(shape, 0, SUB, width)
        turn = index(shape, 0, SUB * width, 2) - index(shape, 1, SUB, 2) + 4
        energy = index(shape, 1, 2 * SUB, groups) * local + j
        fwd_ref[j] = table(shape, lax.rem(point * energy, period), turn, 1.0)

        shape = inv_ref.shape[1:]
        component = index(shape, 0, SUB, 2)
        part = index(shape, 1, SUB * width, 2)
        lag = index(shape, 0, 2 * SUB, groups) * local + j
        other = 1 - component if 2 * j <= local else 3 - component
        turn = jnp.where(part == 0, 3 * component, other)
        point = index(shape, 1, SUB, width)
        inv_ref[j] = table(shape, lax.rem(point * lag, period), turn, 2.0 / period / period)


def negated(x):
    return None if x is None else -x


def scaled(x, factor):
    return None if x is None else x * factor


def turned(value, numerator, denominator):
    re, im = value
    angle = numerator % denominator
    if angle == 0:
        return re, im
    if 2 * angle == denominator:
        return negated(re), negated(im)
    if 4 * angle == denominator:
        return negated(im), re
    if 4 * angle == 3 * denominator:
        return im, negated(re)
    c = math.cos(2.0 * math.pi * angle / denominator)
    s = math.sin(2.0 * math.pi * angle / denominator)
    return added((scaled(re, c), scaled(re, s)), (scaled(im, -s), scaled(im, c)))


def added(left, right):
    def one(x, y):
        return y if x is None else x if y is None else x + y

    return one(left[0], right[0]), one(left[1], right[1])


def short_transform(values, sign):
    count = len(values)
    if count == 1:
        return values
    if count % 2:
        result = []
        for m in range(count):
            total = values[0]
            for j in range(1, count):
                total = added(total, turned(values[j], sign * j * m, count))
            result.append(total)
        return result
    even = short_transform(values[0::2], sign)
    odd = short_transform(values[1::2], sign)
    half = count // 2
    odd = [turned(value, sign * m, count) for m, value in enumerate(odd)]
    minus = [turned(value, 1, 2) for value in odd]
    return [added(e, o) for e, o in zip(even, odd)] + [added(e, o) for e, o in zip(even, minus)]


def dot(left, right):
    return jnp.dot(left, right, preferred_element_type=F32)


def dot_t(left, right):
    return lax.dot_general(left, right, (((1,), (1,)), ((), ())), preferred_element_type=F32)


def beside(left, right):
    return jnp.concatenate([left, right], axis=1)


def above(top, bottom):
    return jnp.concatenate([top, bottom], axis=0)


def sandwich(re, im, negative, middle_re, middle_im):
    middle = above(middle_re, middle_im)
    tr = dot(beside(re, negative), middle).astype(BF16)
    ti = dot(beside(im, re), middle).astype(BF16)
    left = beside(tr, ti)
    return dot_t(left, beside(re, im)), dot_t(left, beside(negative, re))


def kernel(
    groups, slices, cores,
    gd_hbm, gu_hbm, s_hbm, w_hbm, out_ref,
    fwd_ref, inv_ref, gd, gu, sig, scr, snext, loan, own, minus, wminus,
    lbuf, lred, ents, entr, zbuf, qbuf, pbuf, back, rbuf, redp, passed,
    ready, go, in_sem, z_send, z_recv, l_send, l_recv, a_send, a_recv, r_send, r_recv, b_send, b_recv, b_real, d_sem, p_sem,
):
    me = lax.axis_index("energy")
    cut = lax.axis_index("cuts")
    local, _, size, _ = gd.shape
    blocks = lbuf.shape[1]
    extra = (size // SUB - blocks * groups) // cores

    barrier = pltpu.get_barrier_semaphore()

    first = lax.rem(me, 2)
    partner = me + 1 - 2 * first
    last = local - 1

    @pl.when(cut < slices - 1)
    def _():
        for who in (me, partner):
            pl.semaphore_signal(
                barrier, inc=1, device_id={"energy": who, "cuts": cut + 1}, device_id_type=MESH
            )

    pl.semaphore_signal(barrier, inc=1, device_id={"energy": partner}, device_id_type=MESH)

    def to_others(semaphore):
        def greet(k, carry):
            pl.semaphore_signal(semaphore, inc=1, device_id={"energy": k}, device_id_type=MESH)
            return carry

        lax.fori_loop(1, groups, greet, 0)

    @pl.when(me == 0)
    def _():
        to_others(barrier)

    loads = [
        pltpu.make_async_copy(source, target, in_sem.at[i])
        for i, (source, target) in enumerate(
            [(gd_hbm, gd), (s_hbm, sig), (gu_hbm, gu), (w_hbm, scr)]
        )
    ]
    pl.semaphore_wait(
        barrier, 1 + jnp.where(me > 0, 1, 0) + 2 * jnp.where(cut > 0, 1, 0)
    )

    def lend(j):
        return pltpu.make_async_remote_copy(
            src_ref=s_hbm.at[j, 1 - first], dst_ref=loan.at[j],
            send_sem=l_send.at[j], recv_sem=l_recv.at[j],
            device_id={"energy": partner, "cuts": cut}, device_id_type=MESH,
        )

    def shift_mine(j):
        return pltpu.make_async_remote_copy(
            src_ref=s_hbm.at[j, first], dst_ref=snext.at[j, first],
            send_sem=z_send.at[0, j], recv_sem=z_recv.at[0, j],
            device_id={"energy": me, "cuts": cut - 1}, device_id_type=MESH,
        )

    def shift_loan(j):
        return pltpu.make_async_remote_copy(
            src_ref=loan.at[j], dst_ref=snext.at[j, first],
            send_sem=z_send.at[1, j], recv_sem=z_recv.at[1, j],
            device_id={"energy": partner, "cuts": cut - 1}, device_id_type=MESH,
        )

    @pl.when(cut > 0)
    def _():
        shift_mine(0).start()
        for j in range(local):
            lend(j).start()
        lend(0).wait_recv()
        shift_loan(0).start()

        @pl.when(first == 0)
        def _():
            for j in range(1, local):
                shift_mine(j).start()
                lend(j).wait_recv()
                shift_loan(j).start()

        @pl.when(first == 1)
        def _():
            for j in range(1, local):
                lend(j).wait_recv()
                shift_loan(j).start()
                shift_mine(j).start()

    for load in loads:
        load.start()

    @pl.when(me > 0)
    def _():
        pl.semaphore_signal(ready, inc=1, device_id={"energy": 0}, device_id_type=MESH)

    @pl.when(me == 0)
    def _():
        pl.semaphore_wait(ready, groups - 1)
        to_others(go)

    for load in loads:
        load.wait()

    half = 2 * groups * SUB

    def forward(at, j, entries):
        zbuf[at, j] = dot(fwd_ref[j], entries.reshape(half, size))

    def forward_block(j, b):
        wait_for(ents.at[j, b], a_recv.at[j, b])
        forward(b, j, ents[j, b])

    def wait_for(some, semaphore, less=0):
        landed = some.at[pl.ds(0, groups - 1 - less)]
        pltpu.make_async_copy(landed, landed, semaphore).wait()

    def pass_on():
        return pltpu.make_async_remote_copy(
            src_ref=lred.at[last], dst_ref=passed,
            send_sem=p_sem.at[0], recv_sem=p_sem.at[1],
            device_id={"energy": partner}, device_id_type=MESH,
        )

    def each(count, body):
        lax.fori_loop(0, count, lambda b, carry: (body(b), carry)[1], 0)

    def partner_at(k):
        to = me
        bit = 1
        while bit < groups:
            if k & bit:
                to = to + bit - 2 * bit * lax.rem(lax.div(me, bit), 2)
            bit *= 2
        return to

    if groups & (groups - 1):
        targets = [lax.rem(me + k, groups) for k in range(1, groups)]
    else:
        targets = [partner_at(k) for k in range(groups - 1, 0, -1)]

    def lesser_step(j, carry):
        own[0], own[1] = sandwich(gd[j, 0], gd[j, 1], -gd[j, 1], sig[j, 0], sig[j, 1])
        minus[...] = -gu[j, 1]
        wminus[j] = -scr[j, 1]

        @pl.when(j == min(1, last))
        def _():
            fill_tables(fwd_ref, inv_ref, groups, local)

        @pl.when(cut < slices - 1)
        def _():
            shift_mine(j).wait_recv()
            shift_loan(j).wait_recv()
            re, im = sandwich(gu[j, 0], gu[j, 1], minus[...], snext[j, 0], snext[j, 1])
            own[0] += re
            own[1] += im

        for c in range(2):
            value = own[c].astype(BF16).reshape(size // SUB, SUB, size)
            for b in range(blocks):
                lbuf[j, b, :, c] = value[b * groups : (b + 1) * groups]
            for i in range(cores * extra):
                lred[j, i // extra, i % extra, c] = value[blocks * groups + i]

        @pl.when((j == 0) & (me > 0))
        def _():
            pl.semaphore_wait(go, 1)

        def spread(b):
            def send(to):
                pltpu.make_async_remote_copy(
                    src_ref=lbuf.at[j, b, to], dst_ref=ents.at[j, b, me],
                    send_sem=a_send.at[j, b], recv_sem=a_recv.at[j, b],
                    device_id={"energy": to}, device_id_type=MESH,
                ).start()

            for to in targets:
                send(to)
            ents[j, b, me] = lbuf[j, b, me]

        if extra:
            pl.when((j == last) & (first == 1))(lambda: pass_on().start())
        each(blocks, spread)

        def send_extra(to):
            pltpu.make_async_remote_copy(
                src_ref=lred.at[j, lax.rem(to, cores)], dst_ref=entr.at[j, me],
                send_sem=r_send.at[j], recv_sem=r_recv.at[j],
                device_id={"energy": to}, device_id_type=MESH,
            ).start()

        if extra:
            @pl.when((j < last) | (first == 0))
            def _():
                for to in targets:
                    send_extra(to)

            entr[j, me] = lred[j, lax.rem(me, cores)]
        @pl.when(j > 0)
        def _():
            each(blocks, lambda b: forward_block(j - 1, b))
            if extra:
                wait_for(entr.at[j - 1], r_recv.at[j - 1])
                each(extra, lambda i: forward(blocks + i, j - 1, entr[j - 1, :, i]))

        return carry

    lax.fori_loop(0, local, lesser_step, 0)

    if extra:
        @pl.when(first == 0)
        def _():
            pass_on().wait_recv()

            def send_passed(to):
                pltpu.make_async_remote_copy(
                    src_ref=passed.at[lax.rem(to, cores)], dst_ref=entr.at[last, partner],
                    send_sem=p_sem.at[2], recv_sem=r_recv.at[last],
                    device_id={"energy": to}, device_id_type=MESH,
                ).start()

            for to in targets:
                pl.when(to != partner)(functools.partial(send_passed, to))
            entr[last, partner] = passed[0]

    slots = [u if 2 * u <= local else local - u for u in range(local)]
    offset = [max(0, 2 * u - 1) for u in range(local // 2 + 1)]

    def spectrum(block):
        step = 2 * SUB
        for at in range(0, half, step):
            for lane in range(0, size, LANES):
                lanes = slice(lane, lane + LANES)
                z = [
                    (zbuf[block, j, at : at + step, lanes], zbuf[block, j, half + at : half + at + step, lanes])
                    for j in range(local)
                ]
                power = [(re * re + im * im, None) for re, im in short_transform(z, -1)]
                for u, (re, im) in enumerate(short_transform(power, 1)[: local // 2 + 1]):
                    qbuf[offset[u], at : at + step, lanes] = re.astype(BF16)
                    if 0 < 2 * u < local:
                        qbuf[offset[u] + 1, at : at + step, lanes] = im.astype(BF16)

    def lags(u, rows):
        slot = slots[u]
        if 0 < 2 * slot < local:
            q = qbuf[offset[slot] : offset[slot] + 2].reshape(2 * half, size)
            return dot(inv_ref[u, rows, :], q)
        return dot(inv_ref[u, rows, :half], qbuf[offset[slot]])

    def hand_over():
        return pltpu.make_async_remote_copy(
            src_ref=rbuf, dst_ref=redp.at[first],
            send_sem=d_sem.at[0], recv_sem=d_sem.at[1],
            device_id={"energy": partner}, device_id_type=MESH,
        )

    def shared_rows():
        pl.when(first == 0)(lambda: wait_for(entr.at[last], r_recv.at[last], 1))
        pl.when(first == 1)(lambda: wait_for(entr.at[last], r_recv.at[last]))

        def extra_step(i, carry):
            forward(blocks + i, last, entr[last, :, i])
            spectrum(blocks + i)
            step = 2 * SUB
            for u in range(local):
                mine = lags(u, pl.ds(pl.multiple_of(me * step, step), step))
                theirs = lags(u, pl.ds(pl.multiple_of(partner * step, step), step))
                redp[first, u, i] = mine.reshape(2, SUB, size).astype(BF16)
                rbuf[u, i] = theirs.reshape(2, SUB, size).astype(BF16)
            return carry

        lax.fori_loop(0, extra, extra_step, 0)
        hand_over().start()

    def block_step(b, carry):
        if extra:
            pl.when(b == blocks - 1)(shared_rows)

        forward_block(last, b)
        spectrum(b)
        for u in range(local):
            pbuf[b, u] = lags(u, slice(None)).reshape(groups, 2, SUB, size).astype(BF16)

            def send(to):
                pltpu.make_async_remote_copy(
                    src_ref=pbuf.at[b, u, to], dst_ref=back.at[u, b, me],
                    send_sem=b_send.at[b, u], recv_sem=b_recv.at[b, u],
                    device_id={"energy": to}, device_id_type=MESH,
                ).start()

            def send_real():
                pltpu.make_async_remote_copy(
                    src_ref=pbuf.at[b, 0, 0, 0], dst_ref=back.at[0, b, me, 0],
                    send_sem=b_real.at[0, b], recv_sem=b_real.at[1, b],
                    device_id={"energy": 0}, device_id_type=MESH,
                ).start()

            for to in targets:
                if u:
                    send(to)
                else:
                    pl.when(to > 0)(functools.partial(send, to))
                    pl.when(to == 0)(send_real)
            back[u, b, me] = pbuf[b, u, me]
        return carry

    lax.fori_loop(0, blocks, block_step, 0)

    if extra:
        hand_over().wait_recv()

    def result_step(u, carry):
        real_only = (me == 0) & (u == 0)

        @pl.when(real_only)
        def _():
            for b in range(blocks):
                wait_for(back.at[0, b, :, 0], b_real.at[1, b])
                for source in range(groups):
                    back[0, b, source, 1] = jnp.zeros_like(back[0, b, source, 1])

        @pl.when(jnp.logical_not(real_only))
        def _():
            for b in range(blocks):
                wait_for(back.at[u, b], b_recv.at[b, u])

        polar = []
        for c in range(2):
            value = back[u, :, :, c].reshape(blocks * groups * SUB, size)
            if extra:
                value = jnp.concatenate([value, redp[:, u, :, c].reshape(cores * extra * SUB, size)], axis=0)
            polar.append(value)
        re, im = sandwich(scr[u, 0], scr[u, 1], wminus[u], polar[0], polar[1])
        out_ref[u, 0] = re.astype(BF16)
        out_ref[u, 1] = im.astype(BF16)
        return carry

    lax.fori_loop(0, local, result_step, 0)

    @pl.when(cut > 0)
    def _():
        for j in range(local):
            shift_mine(j).wait_send()
            shift_loan(j).wait_send()
            lend(j).wait_send()

    for j in range(local):
        if extra and j < last:
            wait_for(entr.at[j], r_send.at[j])
        for b in range(blocks):
            wait_for(lbuf.at[j, b], a_send.at[j, b])
            if j:
                wait_for(pbuf.at[b, j], b_send.at[b, j])
            else:
                @pl.when(me == 0)
                def _():
                    wait_for(pbuf.at[b, 0], b_send.at[b, 0])

                @pl.when(me > 0)
                def _():
                    other = pbuf.at[b, 0, pl.ds(0, groups - 2)]
                    pltpu.make_async_copy(other, other, b_send.at[b, 0]).wait()
                    real = pbuf.at[b, 0, 0, 0]
                    pltpu.make_async_copy(real, real, b_real.at[0, b]).wait()
    if extra:
        hand_over().wait_send()

        @pl.when(first == 0)
        def _():
            wait_for(entr.at[last], r_send.at[last])
            wait_for(entr.at[last], p_sem.at[2], 1)

        pl.when(first == 1)(lambda: pass_on().wait_send())


def solution(mesh):
    groups, slices = mesh.shape["energy"], mesh.shape["cuts"]
    cores = 2

    def shards(green_diag, green_upper, sigma_lesser, screening):
        shape = green_diag.shape[1:]
        local, _, size, _ = shape
        shared = size // SHARE
        if (size - shared) % (groups * SUB) or shared % (cores * SUB):
            shared = 0
        blocks = (size - shared) // (groups * SUB)
        extra = shared // (cores * SUB)
        some = max(1, extra)
        half = 2 * groups * SUB
        tile = (2, SUB, size)
        block = pltpu.VMEM(shape, BF16)
        dma = pltpu.SemaphoreType.DMA
        anywhere = pl.BlockSpec(memory_space=pltpu.HBM)
        result = pl.pallas_call(
            functools.partial(kernel, groups, slices, cores),
            out_shape=jax.ShapeDtypeStruct(shape, BF16),
            in_specs=[anywhere] * 4,
            out_specs=pl.BlockSpec(memory_space=pltpu.VMEM),
            scratch_shapes=[
                pltpu.VMEM((local, 2 * half, half), BF16),
                pltpu.VMEM((local, half, 2 * half), BF16),
                block, block, block, block, block,
                pltpu.VMEM((local,) + shape[2:], BF16),
                pltpu.VMEM(shape[1:], F32),
                pltpu.VMEM(shape[2:], BF16),
                pltpu.VMEM((local,) + shape[2:], BF16),
                pltpu.VMEM((local, blocks, groups) + tile, BF16),
                pltpu.VMEM((local, cores, some) + tile, BF16),
                pltpu.VMEM((local, blocks, groups) + tile, BF16),
                pltpu.VMEM((local, groups, some) + tile, BF16),
                pltpu.VMEM((blocks + extra, local, 2 * half, size), F32),
                pltpu.VMEM((local, half, size), BF16),
                pltpu.VMEM((blocks, local, groups) + tile, BF16),
                pltpu.VMEM((local, blocks, groups) + tile, BF16),
                pltpu.VMEM((local, some) + tile, BF16),
                pltpu.VMEM((cores, local, some) + tile, BF16),
                pltpu.VMEM((cores, some) + tile, BF16),
                pltpu.SemaphoreType.REGULAR, pltpu.SemaphoreType.REGULAR,
                dma((4,)),
                dma((2, local)), dma((2, local)), dma((local,)), dma((local,)),
                dma((local, blocks)), dma((local, blocks)), dma((local,)), dma((local,)),
                dma((blocks, local)), dma((blocks, local)), dma((2, blocks)), dma((2,)), dma((3,)),
            ],
            compiler_params=pltpu.CompilerParams(
                collective_id=0, has_side_effects=True, vmem_limit_bytes=54525952
            ),
        )(
            green_diag[0], green_upper[0], sigma_lesser[0], screening[0]
        )
        return result[None]

    spec = P("cuts", "energy", None, None, None)
    return jax.shard_map(
        shards, mesh=mesh, in_specs=(spec,) * 4, out_specs=spec, check_vma=False
    )
```

```python
import functools
import math

import jax
import jax.numpy as jnp
from jax import lax
from jax.experimental import pallas as pl
from jax.experimental.pallas import tpu as pltpu
from jax.sharding import PartitionSpec as P

LANES = 128
SUB = 8
SHARE = 4
MESH = pl.DeviceIdType.MESH
F32 = jnp.float32
BF16 = jnp.bfloat16


def fill_tables(fwd_ref, inv_ref, groups, local):
    width = 2 * groups
    period = width * local
    side = max(LANES, 2 * width)

    def index(shape, axis, unit=1, count=None):
        value = lax.div(lax.broadcasted_iota(jnp.int32, shape, axis), unit)
        return value if count is None else lax.rem(value, count)

    def table(phase, quarters, scale):
        turn = lax.rem(phase + quarters * (period // 4), period)
        return (jnp.cos(turn.astype(F32) * (2.0 * math.pi / period)) * scale).astype(BF16)

    def ones(condition):
        return jnp.where(condition, 1.0, 0.0).astype(BF16)

    small = (side, side)

    def expander(shape):
        tall, wide = (shape[0], side), (side, shape[1])
        left = ones(index(tall, 0, SUB) == index(tall, 1))
        right = ones(index(wide, 0) == index(wide, 1, SUB))
        same = index(shape, 0, 1, SUB) == index(shape, 1, 1, SUB)

        def expand(value):
            spread = dot(dot(left, value).astype(BF16), right)
            return jnp.where(same, spread, 0.0).astype(BF16)

        return expand

    expand = expander(fwd_ref.shape[1:])
    for j in range(local):
        point = index(small, 0, 1, width)
        turn = index(small, 0, width, 2) - index(small, 1, 1, 2) + 4
        energy = index(small, 1, 2, groups) * local + j
        fwd_ref[j] = expand(table(lax.rem(point * energy, period), turn, 1.0))

    expand = expander(inv_ref.shape[1:])
    for j in range(local):
        component = index(small, 0, 1, 2)
        part = index(small, 1, width, 2)
        lag = index(small, 0, 2, groups) * local + j
        other = 1 - component if 2 * j <= local else 3 - component
        turn = jnp.where(part == 0, 3 * component, other)
        point = index(small, 1, 1, width)
        inv_ref[j] = expand(table(lax.rem(point * lag, period), turn, 2.0 / period / period))


def negated(x):
    return None if x is None else -x


def scaled(x, factor):
    return None if x is None else x * factor


def turned(value, numerator, denominator):
    re, im = value
    angle = numerator % denominator
    if angle == 0:
        return re, im
    if 2 * angle == denominator:
        return negated(re), negated(im)
    if 4 * angle == denominator:
        return negated(im), re
    if 4 * angle == 3 * denominator:
        return im, negated(re)
    c = math.cos(2.0 * math.pi * angle / denominator)
    s = math.sin(2.0 * math.pi * angle / denominator)
    return added((scaled(re, c), scaled(re, s)), (scaled(im, -s), scaled(im, c)))


def added(left, right):
    def one(x, y):
        return y if x is None else x if y is None else x + y

    return one(left[0], right[0]), one(left[1], right[1])


def short_transform(values, sign):
    count = len(values)
    if count == 1:
        return values
    if count % 2:
        result = []
        for m in range(count):
            total = values[0]
            for j in range(1, count):
                total = added(total, turned(values[j], sign * j * m, count))
            result.append(total)
        return result
    even = short_transform(values[0::2], sign)
    odd = short_transform(values[1::2], sign)
    half = count // 2
    odd = [turned(value, sign * m, count) for m, value in enumerate(odd)]
    minus = [turned(value, 1, 2) for value in odd]
    return [added(e, o) for e, o in zip(even, odd)] + [added(e, o) for e, o in zip(even, minus)]


def dot(left, right):
    return jnp.dot(left, right, preferred_element_type=F32)


def dot_t(left, right):
    return lax.dot_general(left, right, (((1,), (1,)), ((), ())), preferred_element_type=F32)


def beside(left, right):
    return jnp.concatenate([left, right], axis=1)


def above(top, bottom):
    return jnp.concatenate([top, bottom], axis=0)


def sandwich(re, im, negative, middle_re, middle_im):
    middle = above(middle_re, middle_im)
    tr = dot(beside(re, negative), middle).astype(BF16)
    ti = dot(beside(im, re), middle).astype(BF16)
    left = beside(tr, ti)
    return dot_t(left, beside(re, im)), dot_t(left, beside(negative, re))


def kernel(
    groups, slices, cores,
    gd_hbm, gu_hbm, s_hbm, w_hbm, out_ref,
    fwd_ref, inv_ref, gd, gu, sig, scr, snext, loan, own, minus, wminus,
    lbuf, lred, ents, entr, zbuf, qbuf, pbuf, back, rbuf, redp,
    ready, go, in_sem, z_send, z_recv, l_send, l_recv, a_send, a_recv, r_send, r_recv, b_send, b_recv, b_real, d_sem,
):
    me = lax.axis_index("energy")
    cut = lax.axis_index("cuts")
    local, _, size, _ = gd.shape
    blocks = lbuf.shape[1]
    extra = (size // SUB - blocks * groups) // cores

    barrier = pltpu.get_barrier_semaphore()

    first = lax.rem(me, 2)
    partner = me + 1 - 2 * first
    last = local - 1

    @pl.when(cut < slices - 1)
    def _():
        for who in (me, partner):
            pl.semaphore_signal(
                barrier, inc=1, device_id={"energy": who, "cuts": cut + 1}, device_id_type=MESH
            )

    pl.semaphore_signal(barrier, inc=1, device_id={"energy": partner}, device_id_type=MESH)

    def to_others(semaphore):
        def greet(k, carry):
            pl.semaphore_signal(semaphore, inc=1, device_id={"energy": k}, device_id_type=MESH)
            return carry

        lax.fori_loop(1, groups, greet, 0)

    @pl.when(me == 0)
    def _():
        to_others(barrier)

    loads = [
        pltpu.make_async_copy(source, target, in_sem.at[i])
        for i, (source, target) in enumerate(
            [(gd_hbm, gd), (s_hbm, sig), (gu_hbm, gu), (w_hbm, scr)]
        )
    ]
    pl.semaphore_wait(
        barrier, 1 + jnp.where(me > 0, 1, 0) + 2 * jnp.where(cut > 0, 1, 0)
    )

    def lend(j):
        return pltpu.make_async_remote_copy(
            src_ref=s_hbm.at[j, 1 - first], dst_ref=loan.at[j],
            send_sem=l_send.at[j], recv_sem=l_recv.at[j],
            device_id={"energy": partner, "cuts": cut}, device_id_type=MESH,
        )

    def shift_mine(j):
        return pltpu.make_async_remote_copy(
            src_ref=s_hbm.at[j, first], dst_ref=snext.at[j, first],
            send_sem=z_send.at[0, j], recv_sem=z_recv.at[0, j],
            device_id={"energy": me, "cuts": cut - 1}, device_id_type=MESH,
        )

    def shift_loan(j):
        return pltpu.make_async_remote_copy(
            src_ref=loan.at[j], dst_ref=snext.at[j, first],
            send_sem=z_send.at[1, j], recv_sem=z_recv.at[1, j],
            device_id={"energy": partner, "cuts": cut - 1}, device_id_type=MESH,
        )

    @pl.when(cut > 0)
    def _():
        shift_mine(0).start()
        for j in range(local):
            lend(j).start()
        lend(0).wait_recv()
        shift_loan(0).start()

        @pl.when(first == 0)
        def _():
            for j in range(1, local):
                shift_mine(j).start()
                lend(j).wait_recv()
                shift_loan(j).start()

        @pl.when(first == 1)
        def _():
            for j in range(1, local):
                lend(j).wait_recv()
                shift_loan(j).start()
                shift_mine(j).start()

    for load in loads:
        load.start()

    @pl.when(me > 0)
    def _():
        pl.semaphore_signal(ready, inc=1, device_id={"energy": 0}, device_id_type=MESH)

    @pl.when(me == 0)
    def _():
        pl.semaphore_wait(ready, groups - 1)
        to_others(go)

    fill_tables(fwd_ref, inv_ref, groups, local)
    for load in loads:
        load.wait()

    half = 2 * groups * SUB

    def forward(at, j, entries):
        zbuf[at, j] = dot(fwd_ref[j], entries.reshape(half, size))

    def forward_block(j, b):
        wait_for(ents.at[j, b], a_recv.at[j, b])
        forward(b, j, ents[j, b])

    def wait_for(some, semaphore):
        landed = some.at[pl.ds(0, groups - 1)]
        pltpu.make_async_copy(landed, landed, semaphore).wait()

    def each(count, body):
        lax.fori_loop(0, count, lambda b, carry: (body(b), carry)[1], 0)

    def partner_at(k):
        to = me
        bit = 1
        while bit < groups:
            if k & bit:
                to = to + bit - 2 * bit * lax.rem(lax.div(me, bit), 2)
            bit *= 2
        return to

    if groups & (groups - 1):
        targets = [lax.rem(me + k, groups) for k in range(1, groups)]
    else:
        targets = [partner_at(k) for k in range(groups - 1, 0, -1)]

    @pl.when(me == 0)
    def _():
        for b in range(blocks):
            for source in range(groups):
                back[0, b, source, 1] = jnp.zeros(back.shape[4:], BF16)

    def lesser_step(j, carry):
        own[0], own[1] = sandwich(gd[j, 0], gd[j, 1], -gd[j, 1], sig[j, 0], sig[j, 1])
        minus[...] = -gu[j, 1]
        wminus[j] = -scr[j, 1]

        @pl.when(cut < slices - 1)
        def _():
            shift_mine(j).wait_recv()
            shift_loan(j).wait_recv()
            re, im = sandwich(gu[j, 0], gu[j, 1], minus[...], snext[j, 0], snext[j, 1])
            own[0] += re
            own[1] += im

        for c in range(2):
            value = own[c].astype(BF16).reshape(size // SUB, SUB, size)
            for b in range(blocks):
                lbuf[j, b, :, c] = value[b * groups : (b + 1) * groups]
            for i in range(cores * extra):
                lred[j, i // extra, i % extra, c] = value[blocks * groups + i]

        @pl.when((j == 0) & (me > 0))
        def _():
            pl.semaphore_wait(go, 1)

        def spread(b):
            def send(to):
                pltpu.make_async_remote_copy(
                    src_ref=lbuf.at[j, b, to], dst_ref=ents.at[j, b, me],
                    send_sem=a_send.at[j, b], recv_sem=a_recv.at[j, b],
                    device_id={"energy": to}, device_id_type=MESH,
                ).start()

            for to in targets:
                send(to)
            ents[j, b, me] = lbuf[j, b, me]

        each(blocks, spread)

        def send_extra(to):
            pltpu.make_async_remote_copy(
                src_ref=lred.at[j, lax.rem(to, cores)], dst_ref=entr.at[j, me],
                send_sem=r_send.at[j], recv_sem=r_recv.at[j],
                device_id={"energy": to}, device_id_type=MESH,
            ).start()

        if extra:
            for to in targets:
                send_extra(to)
            entr[j, me] = lred[j, lax.rem(me, cores)]
        @pl.when(j > 0)
        def _():
            each(blocks, lambda b: forward_block(j - 1, b))
            if extra:
                wait_for(entr.at[j - 1], r_recv.at[j - 1])
                each(extra, lambda i: forward(blocks + i, j - 1, entr[j - 1, :, i]))

        return carry

    lax.fori_loop(0, local, lesser_step, 0)

    slots = [u if 2 * u <= local else local - u for u in range(local)]
    offset = [max(0, 2 * u - 1) for u in range(local // 2 + 1)]

    def spectrum(block):
        step = 2 * SUB
        for at in range(0, half, step):
            for lane in range(0, size, LANES):
                lanes = slice(lane, lane + LANES)
                z = [
                    (zbuf[block, j, at : at + step, lanes], zbuf[block, j, half + at : half + at + step, lanes])
                    for j in range(local)
                ]
                power = [(re * re + im * im, None) for re, im in short_transform(z, -1)]
                for u, (re, im) in enumerate(short_transform(power, 1)[: local // 2 + 1]):
                    qbuf[offset[u], at : at + step, lanes] = re.astype(BF16)
                    if 0 < 2 * u < local:
                        qbuf[offset[u] + 1, at : at + step, lanes] = im.astype(BF16)

    def lags(u, rows):
        slot = slots[u]
        if 0 < 2 * slot < local:
            q = qbuf[offset[slot] : offset[slot] + 2].reshape(2 * half, size)
            return dot(inv_ref[u, rows, :], q)
        return dot(inv_ref[u, rows, :half], qbuf[offset[slot]])

    def hand_over():
        return pltpu.make_async_remote_copy(
            src_ref=rbuf, dst_ref=redp.at[first],
            send_sem=d_sem.at[0], recv_sem=d_sem.at[1],
            device_id={"energy": partner}, device_id_type=MESH,
        )

    def shared_rows():
        wait_for(entr.at[last], r_recv.at[last])

        def extra_step(i, carry):
            forward(blocks + i, last, entr[last, :, i])
            spectrum(blocks + i)
            step = 2 * SUB
            for u in range(local):
                mine = lags(u, pl.ds(pl.multiple_of(me * step, step), step))
                theirs = lags(u, pl.ds(pl.multiple_of(partner * step, step), step))
                redp[first, u, i] = mine.reshape(2, SUB, size).astype(BF16)
                rbuf[u, i] = theirs.reshape(2, SUB, size).astype(BF16)
            return carry

        lax.fori_loop(0, extra, extra_step, 0)
        hand_over().start()

    def block_step(b, carry):
        if extra:
            pl.when(b == blocks - 1)(shared_rows)

        forward_block(last, b)
        spectrum(b)
        for u in range(local):
            pbuf[b, u] = lags(u, slice(None)).reshape(groups, 2, SUB, size).astype(BF16)

            def send(to):
                pltpu.make_async_remote_copy(
                    src_ref=pbuf.at[b, u, to], dst_ref=back.at[u, b, me],
                    send_sem=b_send.at[b, u], recv_sem=b_recv.at[b, u],
                    device_id={"energy": to}, device_id_type=MESH,
                ).start()

            def send_real():
                pltpu.make_async_remote_copy(
                    src_ref=pbuf.at[b, 0, 0, 0], dst_ref=back.at[0, b, me, 0],
                    send_sem=b_real.at[0, b], recv_sem=b_real.at[1, b],
                    device_id={"energy": 0}, device_id_type=MESH,
                ).start()

            for to in targets:
                if u:
                    send(to)
                else:
                    pl.when(to > 0)(functools.partial(send, to))
                    pl.when(to == 0)(send_real)
            back[u, b, me] = pbuf[b, u, me]
        return carry

    lax.fori_loop(0, blocks, block_step, 0)

    if extra:
        hand_over().wait_recv()

    def result_step(u, carry):
        real_only = (me == 0) & (u == 0)

        @pl.when(real_only)
        def _():
            for b in range(blocks):
                wait_for(back.at[0, b, :, 0], b_real.at[1, b])

        @pl.when(jnp.logical_not(real_only))
        def _():
            for b in range(blocks):
                wait_for(back.at[u, b], b_recv.at[b, u])

        polar = []
        for c in range(2):
            value = back[u, :, :, c].reshape(blocks * groups * SUB, size)
            if extra:
                value = jnp.concatenate([value, redp[:, u, :, c].reshape(cores * extra * SUB, size)], axis=0)
            polar.append(value)
        re, im = sandwich(scr[u, 0], scr[u, 1], wminus[u], polar[0], polar[1])
        out_ref[u, 0] = re.astype(BF16)
        out_ref[u, 1] = im.astype(BF16)
        return carry

    lax.fori_loop(0, local, result_step, 0)

    @pl.when(cut > 0)
    def _():
        for j in range(local):
            shift_mine(j).wait_send()
            shift_loan(j).wait_send()
            lend(j).wait_send()

    for j in range(local):
        if extra:
            wait_for(entr.at[j], r_send.at[j])
        for b in range(blocks):
            wait_for(lbuf.at[j, b], a_send.at[j, b])
            if j:
                wait_for(pbuf.at[b, j], b_send.at[b, j])
            else:
                @pl.when(me == 0)
                def _():
                    wait_for(pbuf.at[b, 0], b_send.at[b, 0])

                @pl.when(me > 0)
                def _():
                    other = pbuf.at[b, 0, pl.ds(0, groups - 2)]
                    pltpu.make_async_copy(other, other, b_send.at[b, 0]).wait()
                    real = pbuf.at[b, 0, 0, 0]
                    pltpu.make_async_copy(real, real, b_real.at[0, b]).wait()
    if extra:
        hand_over().wait_send()


def solution(mesh):
    groups, slices = mesh.shape["energy"], mesh.shape["cuts"]
    cores = 2

    def shards(green_diag, green_upper, sigma_lesser, screening):
        shape = green_diag.shape[1:]
        local, _, size, _ = shape
        shared = size // SHARE
        if (size - shared) % (groups * SUB) or shared % (cores * SUB):
            shared = 0
        blocks = (size - shared) // (groups * SUB)
        extra = shared // (cores * SUB)
        some = max(1, extra)
        half = 2 * groups * SUB
        tile = (2, SUB, size)
        block = pltpu.VMEM(shape, BF16)
        dma = pltpu.SemaphoreType.DMA
        anywhere = pl.BlockSpec(memory_space=pltpu.HBM)
        result = pl.pallas_call(
            functools.partial(kernel, groups, slices, cores),
            out_shape=jax.ShapeDtypeStruct(shape, BF16),
            in_specs=[anywhere] * 4,
            out_specs=pl.BlockSpec(memory_space=pltpu.VMEM),
            scratch_shapes=[
                pltpu.VMEM((local, 2 * half, half), BF16),
                pltpu.VMEM((local, half, 2 * half), BF16),
                block, block, block, block, block,
                pltpu.VMEM((local,) + shape[2:], BF16),
                pltpu.VMEM(shape[1:], F32),
                pltpu.VMEM(shape[2:], BF16),
                pltpu.VMEM((local,) + shape[2:], BF16),
                pltpu.VMEM((local, blocks, groups) + tile, BF16),
                pltpu.VMEM((local, cores, some) + tile, BF16),
                pltpu.VMEM((local, blocks, groups) + tile, BF16),
                pltpu.VMEM((local, groups, some) + tile, BF16),
                pltpu.VMEM((blocks + extra, local, 2 * half, size), F32),
                pltpu.VMEM((local, half, size), BF16),
                pltpu.VMEM((blocks, local, groups) + tile, BF16),
                pltpu.VMEM((local, blocks, groups) + tile, BF16),
                pltpu.VMEM((local, some) + tile, BF16),
                pltpu.VMEM((cores, local, some) + tile, BF16),
                pltpu.SemaphoreType.REGULAR, pltpu.SemaphoreType.REGULAR,
                dma((4,)),
                dma((2, local)), dma((2, local)), dma((local,)), dma((local,)),
                dma((local, blocks)), dma((local, blocks)), dma((local,)), dma((local,)),
                dma((blocks, local)), dma((blocks, local)), dma((2, blocks)), dma((2,)),
            ],
            compiler_params=pltpu.CompilerParams(
                collective_id=0, has_side_effects=True, vmem_limit_bytes=54525952
            ),
        )(
            green_diag[0], green_upper[0], sigma_lesser[0], screening[0]
        )
        return result[None]

    spec = P("cuts", "energy", None, None, None)
    return jax.shard_map(
        shards, mesh=mesh, in_specs=(spec,) * 4, out_specs=spec, check_vma=False
    )
```

```python
import functools
import math

import jax
import jax.numpy as jnp
from jax import lax
from jax.experimental import pallas as pl
from jax.experimental.pallas import tpu as pltpu
from jax.sharding import PartitionSpec as P

LANES = 128
SUB = 8
SHARE = 4
MESH = pl.DeviceIdType.MESH
F32 = jnp.float32
BF16 = jnp.bfloat16


def fill_tables(fwd_ref, inv_ref, groups, local):
    width = 2 * groups
    period = width * local
    side = max(LANES, 2 * width)

    def index(shape, axis, unit=1, count=None):
        value = lax.div(lax.broadcasted_iota(jnp.int32, shape, axis), unit)
        return value if count is None else lax.rem(value, count)

    def table(phase, quarters, scale):
        turn = lax.rem(phase + quarters * (period // 4), period)
        return (jnp.cos(turn.astype(F32) * (2.0 * math.pi / period)) * scale).astype(BF16)

    def ones(condition):
        return jnp.where(condition, 1.0, 0.0).astype(BF16)

    small = (side, side)

    def expander(shape):
        tall, wide = (shape[0], side), (side, shape[1])
        left = ones(index(tall, 0, SUB) == index(tall, 1))
        right = ones(index(wide, 0) == index(wide, 1, SUB))
        same = index(shape, 0, 1, SUB) == index(shape, 1, 1, SUB)

        def expand(value):
            spread = dot(dot(left, value).astype(BF16), right)
            return jnp.where(same, spread, 0.0).astype(BF16)

        return expand

    expand = expander(fwd_ref.shape[1:])
    for j in range(local):
        point = index(small, 0, 1, width)
        turn = index(small, 0, width, 2) - index(small, 1, 1, 2) + 4
        energy = index(small, 1, 2, groups) * local + j
        fwd_ref[j] = expand(table(lax.rem(point * energy, period), turn, 1.0))

    expand = expander(inv_ref.shape[1:])
    for j in range(local):
        component = index(small, 0, 1, 2)
        part = index(small, 1, width, 2)
        lag = index(small, 0, 2, groups) * local + j
        other = 1 - component if 2 * j <= local else 3 - component
        turn = jnp.where(part == 0, 3 * component, other)
        point = index(small, 1, 1, width)
        inv_ref[j] = expand(table(lax.rem(point * lag, period), turn, 2.0 / period / period))


def negated(x):
    return None if x is None else -x


def scaled(x, factor):
    return None if x is None else x * factor


def turned(value, numerator, denominator):
    re, im = value
    angle = numerator % denominator
    if angle == 0:
        return re, im
    if 2 * angle == denominator:
        return negated(re), negated(im)
    if 4 * angle == denominator:
        return negated(im), re
    if 4 * angle == 3 * denominator:
        return im, negated(re)
    c = math.cos(2.0 * math.pi * angle / denominator)
    s = math.sin(2.0 * math.pi * angle / denominator)
    return added((scaled(re, c), scaled(re, s)), (scaled(im, -s), scaled(im, c)))


def added(left, right):
    def one(x, y):
        return y if x is None else x if y is None else x + y

    return one(left[0], right[0]), one(left[1], right[1])


def short_transform(values, sign):
    count = len(values)
    if count == 1:
        return values
    if count % 2:
        result = []
        for m in range(count):
            total = values[0]
            for j in range(1, count):
                total = added(total, turned(values[j], sign * j * m, count))
            result.append(total)
        return result
    even = short_transform(values[0::2], sign)
    odd = short_transform(values[1::2], sign)
    half = count // 2
    odd = [turned(value, sign * m, count) for m, value in enumerate(odd)]
    minus = [turned(value, 1, 2) for value in odd]
    return [added(e, o) for e, o in zip(even, odd)] + [added(e, o) for e, o in zip(even, minus)]


def dot(left, right):
    return jnp.dot(left, right, preferred_element_type=F32)


def dot_t(left, right):
    return lax.dot_general(left, right, (((1,), (1,)), ((), ())), preferred_element_type=F32)


def beside(left, right):
    return jnp.concatenate([left, right], axis=1)


def above(top, bottom):
    return jnp.concatenate([top, bottom], axis=0)


def sandwich(re, im, negative, middle_re, middle_im):
    middle = above(middle_re, middle_im)
    tr = dot(beside(re, negative), middle).astype(BF16)
    ti = dot(beside(im, re), middle).astype(BF16)
    left = beside(tr, ti)
    return dot_t(left, beside(re, im)), dot_t(left, beside(negative, re))


def kernel(
    groups, slices, cores,
    gd_hbm, gu_hbm, s_hbm, w_hbm, out_ref,
    fwd_ref, inv_ref, gd, gu, sig, scr, snext, loan, own, minus, wminus,
    lbuf, lred, ents, entr, zbuf, qbuf, pbuf, back, rbuf, redp,
    ready, go, in_sem, z_send, z_recv, l_send, l_recv, a_send, a_recv, r_send, r_recv, b_send, b_recv, b_real, d_sem,
):
    me = lax.axis_index("energy")
    cut = lax.axis_index("cuts")
    local, _, size, _ = gd.shape
    blocks = lbuf.shape[1]
    extra = (size // SUB - blocks * groups) // cores

    barrier = pltpu.get_barrier_semaphore()

    first = lax.rem(me, 2)
    partner = me + 1 - 2 * first
    last = local - 1

    @pl.when(cut < slices - 1)
    def _():
        for who in (me, partner):
            pl.semaphore_signal(
                barrier, inc=1, device_id={"energy": who, "cuts": cut + 1}, device_id_type=MESH
            )

    pl.semaphore_signal(barrier, inc=1, device_id={"energy": partner}, device_id_type=MESH)

    def to_others(semaphore):
        def greet(k, carry):
            pl.semaphore_signal(semaphore, inc=1, device_id={"energy": k}, device_id_type=MESH)
            return carry

        lax.fori_loop(1, groups, greet, 0)

    @pl.when(me == 0)
    def _():
        to_others(barrier)

    loads = [
        pltpu.make_async_copy(source, target, in_sem.at[i])
        for i, (source, target) in enumerate(
            [(gd_hbm, gd), (s_hbm, sig), (gu_hbm, gu), (w_hbm, scr)]
        )
    ]
    pl.semaphore_wait(
        barrier, 1 + jnp.where(me > 0, 1, 0) + 2 * jnp.where(cut > 0, 1, 0)
    )

    def lend(j):
        return pltpu.make_async_remote_copy(
            src_ref=s_hbm.at[j, 1 - first], dst_ref=loan.at[j],
            send_sem=l_send.at[j], recv_sem=l_recv.at[j],
            device_id={"energy": partner, "cuts": cut}, device_id_type=MESH,
        )

    def shift_mine(j):
        return pltpu.make_async_remote_copy(
            src_ref=s_hbm.at[j, first], dst_ref=snext.at[j, first],
            send_sem=z_send.at[0, j], recv_sem=z_recv.at[0, j],
            device_id={"energy": me, "cuts": cut - 1}, device_id_type=MESH,
        )

    def shift_loan(j):
        return pltpu.make_async_remote_copy(
            src_ref=loan.at[j], dst_ref=snext.at[j, first],
            send_sem=z_send.at[1, j], recv_sem=z_recv.at[1, j],
            device_id={"energy": partner, "cuts": cut - 1}, device_id_type=MESH,
        )

    @pl.when(cut > 0)
    def _():
        shift_mine(0).start()
        for j in range(local):
            lend(j).start()
        lend(0).wait_recv()
        shift_loan(0).start()

        @pl.when(first == 0)
        def _():
            for j in range(1, local):
                shift_mine(j).start()
                lend(j).wait_recv()
                shift_loan(j).start()

        @pl.when(first == 1)
        def _():
            for j in range(1, local):
                lend(j).wait_recv()
                shift_loan(j).start()
                shift_mine(j).start()

    for load in loads:
        load.start()

    @pl.when(me > 0)
    def _():
        pl.semaphore_signal(ready, inc=1, device_id={"energy": 0}, device_id_type=MESH)

    @pl.when(me == 0)
    def _():
        pl.semaphore_wait(ready, groups - 1)
        to_others(go)

    fill_tables(fwd_ref, inv_ref, groups, local)
    for load in loads:
        load.wait()

    half = 2 * groups * SUB

    def forward(at, j, entries):
        zbuf[at, j] = dot(fwd_ref[j], entries.reshape(half, size))

    def forward_block(j, b):
        wait_for(ents.at[j, b], a_recv.at[j, b])
        forward(b, j, ents[j, b])

    def wait_for(some, semaphore):
        landed = some.at[pl.ds(0, groups - 1)]
        pltpu.make_async_copy(landed, landed, semaphore).wait()

    def each(count, body):
        lax.fori_loop(0, count, lambda b, carry: (body(b), carry)[1], 0)

    def partner_at(k):
        to = me
        bit = 1
        while bit < groups:
            if k & bit:
                to = to + bit - 2 * bit * lax.rem(lax.div(me, bit), 2)
            bit *= 2
        return to

    if groups & (groups - 1):
        targets = [lax.rem(me + k, groups) for k in range(1, groups)]
    else:
        targets = [partner_at(k) for k in range(groups - 1, 0, -1)]

    @pl.when(me == 0)
    def _():
        for b in range(blocks):
            for source in range(groups):
                back[0, b, source, 1] = jnp.zeros(back.shape[4:], BF16)

    def lesser_step(j, carry):
        own[0], own[1] = sandwich(gd[j, 0], gd[j, 1], -gd[j, 1], sig[j, 0], sig[j, 1])
        minus[...] = -gu[j, 1]
        wminus[j] = -scr[j, 1]

        def pack(re, im):
            for c, part in enumerate((re, im)):
                value = part.astype(BF16).reshape(size // SUB, SUB, size)
                for b in range(blocks):
                    lbuf[j, b, :, c] = value[b * groups : (b + 1) * groups]
                for i in range(cores * extra):
                    lred[j, i // extra, i % extra, c] = value[blocks * groups + i]

        @pl.when(cut < slices - 1)
        def _():
            shift_mine(j).wait_recv()
            shift_loan(j).wait_recv()
            re, im = sandwich(gu[j, 0], gu[j, 1], minus[...], snext[j, 0], snext[j, 1])
            pack(own[0] + re, own[1] + im)

        @pl.when(cut == slices - 1)
        def _():
            pack(own[0], own[1])

        @pl.when((j == 0) & (me > 0))
        def _():
            pl.semaphore_wait(go, 1)

        def spread(b):
            def send(to):
                pltpu.make_async_remote_copy(
                    src_ref=lbuf.at[j, b, to], dst_ref=ents.at[j, b, me],
                    send_sem=a_send.at[j, b], recv_sem=a_recv.at[j, b],
                    device_id={"energy": to}, device_id_type=MESH,
                ).start()

            for to in targets:
                send(to)
            ents[j, b, me] = lbuf[j, b, me]

        each(blocks, spread)

        def send_extra(to):
            pltpu.make_async_remote_copy(
                src_ref=lred.at[j, lax.rem(to, cores)], dst_ref=entr.at[j, me],
                send_sem=r_send.at[j], recv_sem=r_recv.at[j],
                device_id={"energy": to}, device_id_type=MESH,
            ).start()

        if extra:
            for to in targets:
                send_extra(to)
            entr[j, me] = lred[j, lax.rem(me, cores)]
        @pl.when(j > 0)
        def _():
            each(blocks, lambda b: forward_block(j - 1, b))
            if extra:
                wait_for(entr.at[j - 1], r_recv.at[j - 1])
                each(extra, lambda i: forward(blocks + i, j - 1, entr[j - 1, :, i]))

        return carry

    lax.fori_loop(0, local, lesser_step, 0)

    slots = [u if 2 * u <= local else local - u for u in range(local)]
    offset = [max(0, 2 * u - 1) for u in range(local // 2 + 1)]

    def spectrum(block):
        step = 2 * SUB
        for at in range(0, half, step):
            for lane in range(0, size, LANES):
                lanes = slice(lane, lane + LANES)
                z = [
                    (zbuf[block, j, at : at + step, lanes], zbuf[block, j, half + at : half + at + step, lanes])
                    for j in range(local)
                ]
                power = [(re * re + im * im, None) for re, im in short_transform(z, -1)]
                for u, (re, im) in enumerate(short_transform(power, 1)[: local // 2 + 1]):
                    qbuf[offset[u], at : at + step, lanes] = re.astype(BF16)
                    if 0 < 2 * u < local:
                        qbuf[offset[u] + 1, at : at + step, lanes] = im.astype(BF16)

    def lags(u, rows):
        slot = slots[u]
        if 0 < 2 * slot < local:
            q = qbuf[offset[slot] : offset[slot] + 2].reshape(2 * half, size)
            return dot(inv_ref[u, rows, :], q)
        return dot(inv_ref[u, rows, :half], qbuf[offset[slot]])

    def hand_over():
        return pltpu.make_async_remote_copy(
            src_ref=rbuf, dst_ref=redp.at[first],
            send_sem=d_sem.at[0], recv_sem=d_sem.at[1],
            device_id={"energy": partner}, device_id_type=MESH,
        )

    def shared_rows():
        wait_for(entr.at[last], r_recv.at[last])

        def extra_step(i, carry):
            forward(blocks + i, last, entr[last, :, i])
            spectrum(blocks + i)
            step = 2 * SUB
            for u in range(local):
                mine = lags(u, pl.ds(pl.multiple_of(me * step, step), step))
                theirs = lags(u, pl.ds(pl.multiple_of(partner * step, step), step))
                redp[first, u, i] = mine.reshape(2, SUB, size).astype(BF16)
                rbuf[u, i] = theirs.reshape(2, SUB, size).astype(BF16)
            return carry

        lax.fori_loop(0, extra, extra_step, 0)
        hand_over().start()

    def block_step(b, carry):
        if extra:
            pl.when(b == blocks - 1)(shared_rows)

        forward_block(last, b)
        spectrum(b)
        for u in range(local):
            pbuf[b, u] = lags(u, slice(None)).reshape(groups, 2, SUB, size).astype(BF16)

            def send(to):
                pltpu.make_async_remote_copy(
                    src_ref=pbuf.at[b, u, to], dst_ref=back.at[u, b, me],
                    send_sem=b_send.at[b, u], recv_sem=b_recv.at[b, u],
                    device_id={"energy": to}, device_id_type=MESH,
                ).start()

            def send_real():
                pltpu.make_async_remote_copy(
                    src_ref=pbuf.at[b, 0, 0, 0], dst_ref=back.at[0, b, me, 0],
                    send_sem=b_real.at[0, b], recv_sem=b_real.at[1, b],
                    device_id={"energy": 0}, device_id_type=MESH,
                ).start()

            for to in targets:
                if u:
                    send(to)
                else:
                    pl.when(to > 0)(functools.partial(send, to))
                    pl.when(to == 0)(send_real)
            back[u, b, me] = pbuf[b, u, me]
        return carry

    lax.fori_loop(0, blocks, block_step, 0)

    @pl.when(cut > 0)
    def _():
        for j in range(local):
            shift_mine(j).wait_send()
            shift_loan(j).wait_send()
            lend(j).wait_send()

    for j in range(local):
        if extra:
            wait_for(entr.at[j], r_send.at[j])
        for b in range(blocks):
            wait_for(lbuf.at[j, b], a_send.at[j, b])

    def sent(b):
        for j in range(1, local):
            wait_for(pbuf.at[b, j], b_send.at[b, j])

        @pl.when(me == 0)
        def _():
            wait_for(pbuf.at[b, 0], b_send.at[b, 0])

        @pl.when(me > 0)
        def _():
            other = pbuf.at[b, 0, pl.ds(0, groups - 2)]
            pltpu.make_async_copy(other, other, b_send.at[b, 0]).wait()
            real = pbuf.at[b, 0, 0, 0]
            pltpu.make_async_copy(real, real, b_real.at[0, b]).wait()

    for b in range(blocks - 1):
        sent(b)
    if extra:
        hand_over().wait_send()
        hand_over().wait_recv()

    def result_step(u, carry):
        real_only = (me == 0) & (u == 0)

        @pl.when(real_only)
        def _():
            for b in range(blocks):
                wait_for(back.at[0, b, :, 0], b_real.at[1, b])

        @pl.when(jnp.logical_not(real_only))
        def _():
            for b in range(blocks):
                wait_for(back.at[u, b], b_recv.at[b, u])

        polar = []
        for c in range(2):
            value = back[u, :, :, c].reshape(blocks * groups * SUB, size)
            if extra:
                value = jnp.concatenate([value, redp[:, u, :, c].reshape(cores * extra * SUB, size)], axis=0)
            polar.append(value)
        re, im = sandwich(scr[u, 0], scr[u, 1], wminus[u], polar[0], polar[1])
        out_ref[u, 0] = re.astype(BF16)
        out_ref[u, 1] = im.astype(BF16)
        return carry

    lax.fori_loop(0, local, result_step, 0)

    sent(blocks - 1)


def solution(mesh):
    groups, slices = mesh.shape["energy"], mesh.shape["cuts"]
    cores = 2

    def shards(green_diag, green_upper, sigma_lesser, screening):
        shape = green_diag.shape[1:]
        local, _, size, _ = shape
        shared = size // SHARE
        if (size - shared) % (groups * SUB) or shared % (cores * SUB):
            shared = 0
        blocks = (size - shared) // (groups * SUB)
        extra = shared // (cores * SUB)
        some = max(1, extra)
        half = 2 * groups * SUB
        tile = (2, SUB, size)
        block = pltpu.VMEM(shape, BF16)
        dma = pltpu.SemaphoreType.DMA
        anywhere = pl.BlockSpec(memory_space=pltpu.HBM)
        result = pl.pallas_call(
            functools.partial(kernel, groups, slices, cores),
            out_shape=jax.ShapeDtypeStruct(shape, BF16),
            in_specs=[anywhere] * 4,
            out_specs=pl.BlockSpec(memory_space=pltpu.VMEM),
            scratch_shapes=[
                pltpu.VMEM((local, 2 * half, half), BF16),
                pltpu.VMEM((local, half, 2 * half), BF16),
                block, block, block, block, block,
                pltpu.VMEM((local,) + shape[2:], BF16),
                pltpu.VMEM(shape[1:], F32),
                pltpu.VMEM(shape[2:], BF16),
                pltpu.VMEM((local,) + shape[2:], BF16),
                pltpu.VMEM((local, blocks, groups) + tile, BF16),
                pltpu.VMEM((local, cores, some) + tile, BF16),
                pltpu.VMEM((local, blocks, groups) + tile, BF16),
                pltpu.VMEM((local, groups, some) + tile, BF16),
                pltpu.VMEM((blocks + extra, local, 2 * half, size), F32),
                pltpu.VMEM((local, half, size), BF16),
                pltpu.VMEM((blocks, local, groups) + tile, BF16),
                pltpu.VMEM((local, blocks, groups) + tile, BF16),
                pltpu.VMEM((local, some) + tile, BF16),
                pltpu.VMEM((cores, local, some) + tile, BF16),
                pltpu.SemaphoreType.REGULAR, pltpu.SemaphoreType.REGULAR,
                dma((4,)),
                dma((2, local)), dma((2, local)), dma((local,)), dma((local,)),
                dma((local, blocks)), dma((local, blocks)), dma((local,)), dma((local,)),
                dma((blocks, local)), dma((blocks, local)), dma((2, blocks)), dma((2,)),
            ],
            compiler_params=pltpu.CompilerParams(
                collective_id=0, has_side_effects=True, vmem_limit_bytes=54525952
            ),
        )(
            green_diag[0], green_upper[0], sigma_lesser[0], screening[0]
        )
        return result[None]

    spec = P("cuts", "energy", None, None, None)
    return jax.shard_map(
        shards, mesh=mesh, in_specs=(spec,) * 4, out_specs=spec, check_vma=False
    )
```

```python
import functools
import math

import jax
import jax.numpy as jnp
from jax import lax
from jax.experimental import pallas as pl
from jax.experimental.pallas import tpu as pltpu
from jax.sharding import PartitionSpec as P

LANES = 128
SUB = 8
SHARE = 4
MESH = pl.DeviceIdType.MESH
F32 = jnp.float32
BF16 = jnp.bfloat16


def fill_tables(fwd_ref, inv_ref, groups, local):
    width = 2 * groups
    period = width * local
    side = max(LANES, 2 * width)

    def index(shape, axis, unit=1, count=None):
        value = lax.div(lax.broadcasted_iota(jnp.int32, shape, axis), unit)
        return value if count is None else lax.rem(value, count)

    def table(phase, quarters, scale):
        turn = lax.rem(phase + quarters * (period // 4), period)
        return (jnp.cos(turn.astype(F32) * (2.0 * math.pi / period)) * scale).astype(BF16)

    def ones(condition):
        return jnp.where(condition, 1.0, 0.0).astype(BF16)

    small = (side, side)

    def expander(shape):
        tall, wide = (shape[0], side), (side, shape[1])
        left = ones(index(tall, 0, SUB) == index(tall, 1))
        right = ones(index(wide, 0) == index(wide, 1, SUB))
        same = index(shape, 0, 1, SUB) == index(shape, 1, 1, SUB)

        def expand(value):
            spread = dot(dot(left, value).astype(BF16), right)
            return jnp.where(same, spread, 0.0).astype(BF16)

        return expand

    expand = expander(fwd_ref.shape[1:])
    for j in range(local):
        point = index(small, 0, 1, width)
        turn = index(small, 0, width, 2) - index(small, 1, 1, 2) + 4
        energy = index(small, 1, 2, groups) * local + j
        fwd_ref[j] = expand(table(lax.rem(point * energy, period), turn, 1.0))

    expand = expander(inv_ref.shape[1:])
    for j in range(local):
        component = index(small, 0, 1, 2)
        part = index(small, 1, width, 2)
        lag = index(small, 0, 2, groups) * local + j
        other = 1 - component if 2 * j <= local else 3 - component
        turn = jnp.where(part == 0, 3 * component, other)
        point = index(small, 1, 1, width)
        inv_ref[j] = expand(table(lax.rem(point * lag, period), turn, 2.0 / period / period))


def negated(x):
    return None if x is None else -x


def scaled(x, factor):
    return None if x is None else x * factor


def turned(value, numerator, denominator):
    re, im = value
    angle = numerator % denominator
    if angle == 0:
        return re, im
    if 2 * angle == denominator:
        return negated(re), negated(im)
    if 4 * angle == denominator:
        return negated(im), re
    if 4 * angle == 3 * denominator:
        return im, negated(re)
    c = math.cos(2.0 * math.pi * angle / denominator)
    s = math.sin(2.0 * math.pi * angle / denominator)
    return added((scaled(re, c), scaled(re, s)), (scaled(im, -s), scaled(im, c)))


def added(left, right):
    def one(x, y):
        return y if x is None else x if y is None else x + y

    return one(left[0], right[0]), one(left[1], right[1])


def short_transform(values, sign):
    count = len(values)
    if count == 1:
        return values
    if count % 2:
        result = []
        for m in range(count):
            total = values[0]
            for j in range(1, count):
                total = added(total, turned(values[j], sign * j * m, count))
            result.append(total)
        return result
    even = short_transform(values[0::2], sign)
    odd = short_transform(values[1::2], sign)
    half = count // 2
    odd = [turned(value, sign * m, count) for m, value in enumerate(odd)]
    minus = [turned(value, 1, 2) for value in odd]
    return [added(e, o) for e, o in zip(even, odd)] + [added(e, o) for e, o in zip(even, minus)]


def dot(left, right):
    return jnp.dot(left, right, preferred_element_type=F32)


def dot_t(left, right):
    return lax.dot_general(left, right, (((1,), (1,)), ((), ())), preferred_element_type=F32)


def beside(left, right):
    return jnp.concatenate([left, right], axis=1)


def above(top, bottom):
    return jnp.concatenate([top, bottom], axis=0)


def product(re, im, negative, middle_re, middle_im):
    middle = above(middle_re, middle_im)
    return dot(beside(re, negative), middle), dot(beside(im, re), middle)


def adjoint_product(tr, ti, re, im, negative):
    left = beside(tr.astype(BF16), ti.astype(BF16))
    return dot_t(left, beside(re, im)), dot_t(left, beside(negative, re))


def sandwich(re, im, negative, middle_re, middle_im):
    tr, ti = product(re, im, negative, middle_re, middle_im)
    return adjoint_product(tr, ti, re, im, negative)


def kernel(
    groups, slices, cores,
    gd_hbm, gu_hbm, s_hbm, w_hbm, out_ref,
    fwd_ref, inv_ref, gd, gu, sig, scr, snext, loan, own, part, minus, wminus,
    lbuf, lred, ents, entr, zbuf, qbuf, pbuf, back, rbuf, redp,
    ready, go, in_sem, z_send, z_recv, l_send, l_recv, a_send, a_recv, r_send, r_recv, b_send, b_recv, b_real, d_sem,
):
    me = lax.axis_index("energy")
    cut = lax.axis_index("cuts")
    local, _, size, _ = gd.shape
    blocks = lbuf.shape[1]
    extra = (size // SUB - blocks * groups) // cores

    barrier = pltpu.get_barrier_semaphore()

    first = lax.rem(me, 2)
    partner = me + 1 - 2 * first
    last = local - 1

    @pl.when(cut < slices - 1)
    def _():
        for who in (me, partner):
            pl.semaphore_signal(
                barrier, inc=1, device_id={"energy": who, "cuts": cut + 1}, device_id_type=MESH
            )

    pl.semaphore_signal(barrier, inc=1, device_id={"energy": partner}, device_id_type=MESH)

    def to_others(semaphore):
        def greet(k, carry):
            pl.semaphore_signal(semaphore, inc=1, device_id={"energy": k}, device_id_type=MESH)
            return carry

        lax.fori_loop(1, groups, greet, 0)

    @pl.when(me == 0)
    def _():
        to_others(barrier)

    loads = [
        pltpu.make_async_copy(source, target, in_sem.at[i])
        for i, (source, target) in enumerate(
            [(gd_hbm, gd), (s_hbm, sig), (gu_hbm, gu), (w_hbm, scr)]
        )
    ]
    pl.semaphore_wait(
        barrier, 1 + jnp.where(me > 0, 1, 0) + 2 * jnp.where(cut > 0, 1, 0)
    )

    def lend(j):
        return pltpu.make_async_remote_copy(
            src_ref=s_hbm.at[j, 1 - first], dst_ref=loan.at[j],
            send_sem=l_send.at[j], recv_sem=l_recv.at[j],
            device_id={"energy": partner, "cuts": cut}, device_id_type=MESH,
        )

    def shift_mine(j):
        return pltpu.make_async_remote_copy(
            src_ref=s_hbm.at[j, first], dst_ref=snext.at[j, first],
            send_sem=z_send.at[0, j], recv_sem=z_recv.at[0, j],
            device_id={"energy": me, "cuts": cut - 1}, device_id_type=MESH,
        )

    def shift_loan(j):
        return pltpu.make_async_remote_copy(
            src_ref=loan.at[j], dst_ref=snext.at[j, first],
            send_sem=z_send.at[1, j], recv_sem=z_recv.at[1, j],
            device_id={"energy": partner, "cuts": cut - 1}, device_id_type=MESH,
        )

    @pl.when(cut > 0)
    def _():
        shift_mine(0).start()
        for j in range(local):
            lend(j).start()
        lend(0).wait_recv()
        shift_loan(0).start()

        @pl.when(first == 0)
        def _():
            for j in range(1, local):
                shift_mine(j).start()
                lend(j).wait_recv()
                shift_loan(j).start()

        @pl.when(first == 1)
        def _():
            for j in range(1, local):
                lend(j).wait_recv()
                shift_loan(j).start()
                shift_mine(j).start()

    for load in loads:
        load.start()

    @pl.when(me > 0)
    def _():
        pl.semaphore_signal(ready, inc=1, device_id={"energy": 0}, device_id_type=MESH)

    @pl.when(me == 0)
    def _():
        pl.semaphore_wait(ready, groups - 1)
        to_others(go)

    fill_tables(fwd_ref, inv_ref, groups, local)
    for load in loads:
        load.wait()

    half = 2 * groups * SUB

    def forward(at, j, entries):
        zbuf[at, j] = dot(fwd_ref[j], entries.reshape(half, size))

    def forward_block(j, b):
        wait_for(ents.at[j, b], a_recv.at[j, b])
        forward(b, j, ents[j, b])

    def wait_for(some, semaphore):
        landed = some.at[pl.ds(0, groups - 1)]
        pltpu.make_async_copy(landed, landed, semaphore).wait()

    def each(count, body):
        lax.fori_loop(0, count, lambda b, carry: (body(b), carry)[1], 0)

    def partner_at(k):
        to = me
        bit = 1
        while bit < groups:
            if k & bit:
                to = to + bit - 2 * bit * lax.rem(lax.div(me, bit), 2)
            bit *= 2
        return to

    if groups & (groups - 1):
        targets = [lax.rem(me + k, groups) for k in range(1, groups)]
    else:
        targets = [partner_at(k) for k in range(groups - 1, 0, -1)]

    @pl.when(me == 0)
    def _():
        for b in range(blocks):
            for source in range(groups):
                back[0, b, source, 1] = jnp.zeros(back.shape[4:], BF16)

    def lesser_step(j, carry):
        own[0], own[1] = sandwich(gd[j, 0], gd[j, 1], -gd[j, 1], sig[j, 0], sig[j, 1])
        minus[...] = -gu[j, 1]
        wminus[j] = -scr[j, 1]

        def pack(re, im):
            for c, part in enumerate((re, im)):
                value = part.astype(BF16).reshape(size // SUB, SUB, size)
                for b in range(blocks):
                    lbuf[j, b, :, c] = value[b * groups : (b + 1) * groups]
                for i in range(cores * extra):
                    lred[j, i // extra, i % extra, c] = value[blocks * groups + i]

        @pl.when(cut < slices - 1)
        def _():
            shift_mine(j).wait_recv()
            shift_loan(j).wait_recv()
            re, im = sandwich(gu[j, 0], gu[j, 1], minus[...], snext[j, 0], snext[j, 1])
            pack(own[0] + re, own[1] + im)

        @pl.when(cut == slices - 1)
        def _():
            pack(own[0], own[1])

        @pl.when((j == 0) & (me > 0))
        def _():
            pl.semaphore_wait(go, 1)

        def spread(b):
            def send(to):
                pltpu.make_async_remote_copy(
                    src_ref=lbuf.at[j, b, to], dst_ref=ents.at[j, b, me],
                    send_sem=a_send.at[j, b], recv_sem=a_recv.at[j, b],
                    device_id={"energy": to}, device_id_type=MESH,
                ).start()

            for to in targets:
                send(to)
            ents[j, b, me] = lbuf[j, b, me]

        each(blocks, spread)

        def send_extra(to):
            pltpu.make_async_remote_copy(
                src_ref=lred.at[j, lax.rem(to, cores)], dst_ref=entr.at[j, me],
                send_sem=r_send.at[j], recv_sem=r_recv.at[j],
                device_id={"energy": to}, device_id_type=MESH,
            ).start()

        if extra:
            for to in targets:
                send_extra(to)
            entr[j, me] = lred[j, lax.rem(me, cores)]
        @pl.when(j > 0)
        def _():
            each(blocks, lambda b: forward_block(j - 1, b))
            if extra:
                wait_for(entr.at[j - 1], r_recv.at[j - 1])
                each(extra, lambda i: forward(blocks + i, j - 1, entr[j - 1, :, i]))

        return carry

    lax.fori_loop(0, local, lesser_step, 0)

    slots = [u if 2 * u <= local else local - u for u in range(local)]
    offset = [max(0, 2 * u - 1) for u in range(local // 2 + 1)]

    def spectrum(block):
        step = 2 * SUB
        for at in range(0, half, step):
            for lane in range(0, size, LANES):
                lanes = slice(lane, lane + LANES)
                z = [
                    (zbuf[block, j, at : at + step, lanes], zbuf[block, j, half + at : half + at + step, lanes])
                    for j in range(local)
                ]
                power = [(re * re + im * im, None) for re, im in short_transform(z, -1)]
                for u, (re, im) in enumerate(short_transform(power, 1)[: local // 2 + 1]):
                    qbuf[offset[u], at : at + step, lanes] = re.astype(BF16)
                    if 0 < 2 * u < local:
                        qbuf[offset[u] + 1, at : at + step, lanes] = im.astype(BF16)

    def lags(u, rows):
        slot = slots[u]
        if 0 < 2 * slot < local:
            q = qbuf[offset[slot] : offset[slot] + 2].reshape(2 * half, size)
            return dot(inv_ref[u, rows, :], q)
        return dot(inv_ref[u, rows, :half], qbuf[offset[slot]])

    def hand_over():
        return pltpu.make_async_remote_copy(
            src_ref=rbuf, dst_ref=redp.at[first],
            send_sem=d_sem.at[0], recv_sem=d_sem.at[1],
            device_id={"energy": partner}, device_id_type=MESH,
        )

    def shared_rows():
        wait_for(entr.at[last], r_recv.at[last])

        def extra_step(i, carry):
            forward(blocks + i, last, entr[last, :, i])
            spectrum(blocks + i)
            step = 2 * SUB
            for u in range(local):
                mine = lags(u, pl.ds(pl.multiple_of(me * step, step), step))
                theirs = lags(u, pl.ds(pl.multiple_of(partner * step, step), step))
                redp[first, u, i] = mine.reshape(2, SUB, size).astype(BF16)
                rbuf[u, i] = theirs.reshape(2, SUB, size).astype(BF16)
            return carry

        lax.fori_loop(0, extra, extra_step, 0)
        hand_over().start()

    def block_step(b, carry):
        if extra:
            pl.when(b == blocks - 1)(shared_rows)

        forward_block(last, b)
        spectrum(b)
        for u in range(local):
            pbuf[b, u] = lags(u, slice(None)).reshape(groups, 2, SUB, size).astype(BF16)

            def send(to):
                pltpu.make_async_remote_copy(
                    src_ref=pbuf.at[b, u, to], dst_ref=back.at[u, b, me],
                    send_sem=b_send.at[b, u], recv_sem=b_recv.at[b, u],
                    device_id={"energy": to}, device_id_type=MESH,
                ).start()

            def send_real():
                pltpu.make_async_remote_copy(
                    src_ref=pbuf.at[b, 0, 0, 0], dst_ref=back.at[0, b, me, 0],
                    send_sem=b_real.at[0, b], recv_sem=b_real.at[1, b],
                    device_id={"energy": 0}, device_id_type=MESH,
                ).start()

            for to in targets:
                if u:
                    send(to)
                else:
                    pl.when(to > 0)(functools.partial(send, to))
                    pl.when(to == 0)(send_real)
            back[u, b, me] = pbuf[b, u, me]
        return carry

    lax.fori_loop(0, blocks, block_step, 0)

    @pl.when(cut > 0)
    def _():
        for j in range(local):
            shift_mine(j).wait_send()
            shift_loan(j).wait_send()
            lend(j).wait_send()

    for j in range(local):
        if extra:
            wait_for(entr.at[j], r_send.at[j])
        for b in range(blocks):
            wait_for(lbuf.at[j, b], a_send.at[j, b])

    def sent(b):
        for j in range(1, local):
            wait_for(pbuf.at[b, j], b_send.at[b, j])

        @pl.when(me == 0)
        def _():
            wait_for(pbuf.at[b, 0], b_send.at[b, 0])

        @pl.when(me > 0)
        def _():
            other = pbuf.at[b, 0, pl.ds(0, groups - 2)]
            pltpu.make_async_copy(other, other, b_send.at[b, 0]).wait()
            real = pbuf.at[b, 0, 0, 0]
            pltpu.make_async_copy(real, real, b_real.at[0, b]).wait()

    ahead = blocks - 1
    depth = ahead * groups * SUB
    if depth % LANES:
        ahead = depth = 0

    def returned(u, some):
        real_only = (me == 0) & (u == 0)

        @pl.when(real_only)
        def _():
            for b in some:
                wait_for(back.at[0, b, :, 0], b_real.at[1, b])

        @pl.when(jnp.logical_not(real_only))
        def _():
            for b in some:
                wait_for(back.at[u, b], b_recv.at[b, u])

    def screen(u, columns):
        return scr[u, 0, :, columns], scr[u, 1, :, columns], wminus[u, :, columns]

    def early_product(u):
        returned(u, range(ahead))
        polar = [back[u, :ahead, :, c].reshape(depth, size) for c in range(2)]
        part[u, 0], part[u, 1] = product(*screen(u, slice(0, depth)), *polar)

    if ahead:
        each(local, early_product)

    for b in range(blocks - 1):
        sent(b)
    if extra:
        hand_over().wait_send()
        hand_over().wait_recv()

    def result_step(u, carry):
        returned(u, range(ahead, blocks))
        polar = []
        for c in range(2):
            value = back[u, ahead:, :, c].reshape((blocks - ahead) * groups * SUB, size)
            if extra:
                value = above(value, redp[:, u, :, c].reshape(cores * extra * SUB, size))
            polar.append(value)
        tr, ti = product(*screen(u, slice(depth, size)), *polar)
        if ahead:
            tr, ti = part[u, 0] + tr, part[u, 1] + ti
        re, im = adjoint_product(tr, ti, scr[u, 0], scr[u, 1], wminus[u])
        out_ref[u, 0] = re.astype(BF16)
        out_ref[u, 1] = im.astype(BF16)
        return carry

    lax.fori_loop(0, local, result_step, 0)

    sent(blocks - 1)


def solution(mesh):
    groups, slices = mesh.shape["energy"], mesh.shape["cuts"]
    cores = 2

    def shards(green_diag, green_upper, sigma_lesser, screening):
        shape = green_diag.shape[1:]
        local, _, size, _ = shape
        shared = size // SHARE
        if (size - shared) % (groups * SUB) or shared % (cores * SUB):
            shared = 0
        blocks = (size - shared) // (groups * SUB)
        extra = shared // (cores * SUB)
        some = max(1, extra)
        half = 2 * groups * SUB
        tile = (2, SUB, size)
        block = pltpu.VMEM(shape, BF16)
        dma = pltpu.SemaphoreType.DMA
        anywhere = pl.BlockSpec(memory_space=pltpu.HBM)
        result = pl.pallas_call(
            functools.partial(kernel, groups, slices, cores),
            out_shape=jax.ShapeDtypeStruct(shape, BF16),
            in_specs=[anywhere] * 4,
            out_specs=pl.BlockSpec(memory_space=pltpu.VMEM),
            scratch_shapes=[
                pltpu.VMEM((local, 2 * half, half), BF16),
                pltpu.VMEM((local, half, 2 * half), BF16),
                block, block, block, block, block,
                pltpu.VMEM((local,) + shape[2:], BF16),
                pltpu.VMEM(shape[1:], F32),
                pltpu.VMEM(shape, F32),
                pltpu.VMEM(shape[2:], BF16),
                pltpu.VMEM((local,) + shape[2:], BF16),
                pltpu.VMEM((local, blocks, groups) + tile, BF16),
                pltpu.VMEM((local, cores, some) + tile, BF16),
                pltpu.VMEM((local, blocks, groups) + tile, BF16),
                pltpu.VMEM((local, groups, some) + tile, BF16),
                pltpu.VMEM((blocks + extra, local, 2 * half, size), F32),
                pltpu.VMEM((local, half, size), BF16),
                pltpu.VMEM((blocks, local, groups) + tile, BF16),
                pltpu.VMEM((local, blocks, groups) + tile, BF16),
                pltpu.VMEM((local, some) + tile, BF16),
                pltpu.VMEM((cores, local, some) + tile, BF16),
                pltpu.SemaphoreType.REGULAR, pltpu.SemaphoreType.REGULAR,
                dma((4,)),
                dma((2, local)), dma((2, local)), dma((local,)), dma((local,)),
                dma((local, blocks)), dma((local, blocks)), dma((local,)), dma((local,)),
                dma((blocks, local)), dma((blocks, local)), dma((2, blocks)), dma((2,)),
            ],
            compiler_params=pltpu.CompilerParams(
                collective_id=0, has_side_effects=True, vmem_limit_bytes=54525952
            ),
        )(
            green_diag[0], green_upper[0], sigma_lesser[0], screening[0]
        )
        return result[None]

    spec = P("cuts", "energy", None, None, None)
    return jax.shard_map(
        shards, mesh=mesh, in_specs=(spec,) * 4, out_specs=spec, check_vma=False
    )
```

```python
import functools
import math

import jax
import jax.numpy as jnp
from jax import lax
from jax.experimental import pallas as pl
from jax.experimental.pallas import tpu as pltpu
from jax.sharding import PartitionSpec as P

LANES = 128
SUB = 8
SHARE = 4
MESH = pl.DeviceIdType.MESH
F32 = jnp.float32
BF16 = jnp.bfloat16


def fill_tables(fwd_ref, inv_ref, groups, local):
    width = 2 * groups
    period = width * local
    side = max(LANES, 2 * width)

    def index(shape, axis, unit=1, count=None):
        value = lax.div(lax.broadcasted_iota(jnp.int32, shape, axis), unit)
        return value if count is None else lax.rem(value, count)

    def table(phase, quarters, scale):
        turn = lax.rem(phase + quarters * (period // 4), period)
        return (jnp.cos(turn.astype(F32) * (2.0 * math.pi / period)) * scale).astype(BF16)

    def ones(condition):
        return jnp.where(condition, 1.0, 0.0).astype(BF16)

    small = (side, side)

    def expander(shape):
        tall, wide = (shape[0], side), (side, shape[1])
        left = ones(index(tall, 0, SUB) == index(tall, 1))
        right = ones(index(wide, 0) == index(wide, 1, SUB))
        same = index(shape, 0, 1, SUB) == index(shape, 1, 1, SUB)

        def expand(value):
            spread = dot(dot(left, value).astype(BF16), right)
            return jnp.where(same, spread, 0.0).astype(BF16)

        return expand

    expand = expander(fwd_ref.shape[1:])
    for j in range(local):
        point = index(small, 0, 1, width)
        turn = index(small, 0, width, 2) - index(small, 1, 1, 2) + 4
        energy = index(small, 1, 2, groups) * local + j
        fwd_ref[j] = expand(table(lax.rem(point * energy, period), turn, 1.0))

    expand = expander(inv_ref.shape[1:])
    for j in range(local):
        component = index(small, 0, 1, 2)
        part = index(small, 1, width, 2)
        lag = index(small, 0, 2, groups) * local + j
        other = 1 - component if 2 * j <= local else 3 - component
        turn = jnp.where(part == 0, 3 * component, other)
        point = index(small, 1, 1, width)
        inv_ref[j] = expand(table(lax.rem(point * lag, period), turn, 2.0 / period / period))


def negated(x):
    return None if x is None else -x


def scaled(x, factor):
    return None if x is None else x * factor


def turned(value, numerator, denominator):
    re, im = value
    angle = numerator % denominator
    if angle == 0:
        return re, im
    if 2 * angle == denominator:
        return negated(re), negated(im)
    if 4 * angle == denominator:
        return negated(im), re
    if 4 * angle == 3 * denominator:
        return im, negated(re)
    c = math.cos(2.0 * math.pi * angle / denominator)
    s = math.sin(2.0 * math.pi * angle / denominator)
    return added((scaled(re, c), scaled(re, s)), (scaled(im, -s), scaled(im, c)))


def added(left, right):
    def one(x, y):
        return y if x is None else x if y is None else x + y

    return one(left[0], right[0]), one(left[1], right[1])


def short_transform(values, sign):
    count = len(values)
    if count == 1:
        return values
    if count % 2:
        result = []
        for m in range(count):
            total = values[0]
            for j in range(1, count):
                total = added(total, turned(values[j], sign * j * m, count))
            result.append(total)
        return result
    even = short_transform(values[0::2], sign)
    odd = short_transform(values[1::2], sign)
    half = count // 2
    odd = [turned(value, sign * m, count) for m, value in enumerate(odd)]
    minus = [turned(value, 1, 2) for value in odd]
    return [added(e, o) for e, o in zip(even, odd)] + [added(e, o) for e, o in zip(even, minus)]


def dot(left, right):
    return jnp.dot(left, right, preferred_element_type=F32)


def dot_t(left, right):
    return lax.dot_general(left, right, (((1,), (1,)), ((), ())), preferred_element_type=F32)


def beside(left, right):
    return jnp.concatenate([left, right], axis=1)


def above(top, bottom):
    return jnp.concatenate([top, bottom], axis=0)


def product(re, im, negative, middle_re, middle_im):
    middle = above(middle_re, middle_im)
    return dot(beside(re, negative), middle), dot(beside(im, re), middle)


def adjoint_product(tr, ti, re, im, negative):
    left = beside(tr.astype(BF16), ti.astype(BF16))
    return dot_t(left, beside(re, im)), dot_t(left, beside(negative, re))


def sandwich(re, im, negative, middle_re, middle_im):
    tr, ti = product(re, im, negative, middle_re, middle_im)
    return adjoint_product(tr, ti, re, im, negative)


def kernel(
    groups, slices, cores,
    gd_hbm, gu_hbm, s_hbm, w_hbm, out_ref,
    fwd_ref, inv_ref, gd, gu, sig, scr, snext, loan, own, part, minus, wminus,
    lbuf, lred, ents, entr, zbuf, qbuf, pbuf, back, rbuf, redp,
    ready, go, in_sem, z_send, z_recv, l_send, l_recv, a_send, a_recv, r_send, r_recv, b_send, b_recv, b_real, d_sem,
):
    me = lax.axis_index("energy")
    cut = lax.axis_index("cuts")
    local, _, size, _ = gd.shape
    blocks = lbuf.shape[1]
    extra = (size // SUB - blocks * groups) // cores

    barrier = pltpu.get_barrier_semaphore()

    first = lax.rem(me, 2)
    partner = me + 1 - 2 * first
    last = local - 1

    @pl.when(cut < slices - 1)
    def _():
        for who in (me, partner):
            pl.semaphore_signal(
                barrier, inc=1, device_id={"energy": who, "cuts": cut + 1}, device_id_type=MESH
            )

    pl.semaphore_signal(barrier, inc=1, device_id={"energy": partner}, device_id_type=MESH)

    def to_others(semaphore):
        def greet(k, carry):
            pl.semaphore_signal(semaphore, inc=1, device_id={"energy": k}, device_id_type=MESH)
            return carry

        lax.fori_loop(1, groups, greet, 0)

    @pl.when(me == 0)
    def _():
        to_others(barrier)

    loads = [
        pltpu.make_async_copy(source, target, in_sem.at[i])
        for i, (source, target) in enumerate(
            [(gd_hbm, gd), (s_hbm, sig), (gu_hbm, gu), (w_hbm, scr)]
        )
    ]
    pl.semaphore_wait(
        barrier, 1 + jnp.where(me > 0, 1, 0) + 2 * jnp.where(cut > 0, 1, 0)
    )

    def lend(j):
        return pltpu.make_async_remote_copy(
            src_ref=s_hbm.at[j, 1 - first], dst_ref=loan.at[j],
            send_sem=l_send.at[j], recv_sem=l_recv.at[j],
            device_id={"energy": partner, "cuts": cut}, device_id_type=MESH,
        )

    def shift_mine(j):
        return pltpu.make_async_remote_copy(
            src_ref=s_hbm.at[j, first], dst_ref=snext.at[j, first],
            send_sem=z_send.at[0, j], recv_sem=z_recv.at[0, j],
            device_id={"energy": me, "cuts": cut - 1}, device_id_type=MESH,
        )

    def shift_loan(j):
        return pltpu.make_async_remote_copy(
            src_ref=loan.at[j], dst_ref=snext.at[j, first],
            send_sem=z_send.at[1, j], recv_sem=z_recv.at[1, j],
            device_id={"energy": partner, "cuts": cut - 1}, device_id_type=MESH,
        )

    @pl.when(cut > 0)
    def _():
        shift_mine(0).start()
        for j in range(local):
            lend(j).start()
        lend(0).wait_recv()
        shift_loan(0).start()

        @pl.when(first == 0)
        def _():
            for j in range(1, local):
                shift_mine(j).start()
                lend(j).wait_recv()
                shift_loan(j).start()

        @pl.when(first == 1)
        def _():
            for j in range(1, local):
                lend(j).wait_recv()
                shift_loan(j).start()
                shift_mine(j).start()

    for load in loads:
        load.start()

    @pl.when(me > 0)
    def _():
        pl.semaphore_signal(ready, inc=1, device_id={"energy": 0}, device_id_type=MESH)

    @pl.when(me == 0)
    def _():
        pl.semaphore_wait(ready, groups - 1)
        to_others(go)

    fill_tables(fwd_ref, inv_ref, groups, local)
    for load in loads:
        load.wait()

    half = 2 * groups * SUB

    def forward(at, j, entries):
        zbuf[at, j] = dot(fwd_ref[j], entries.reshape(half, size))

    def forward_block(j, b):
        wait_for(ents.at[j, b], a_recv.at[j, b])
        forward(b, j, ents[j, b])

    def wait_for(some, semaphore):
        landed = some.at[pl.ds(0, groups - 1)]
        pltpu.make_async_copy(landed, landed, semaphore).wait()

    def each(count, body):
        lax.fori_loop(0, count, lambda b, carry: (body(b), carry)[1], 0)

    def partner_at(k):
        to = me
        bit = 1
        while bit < groups:
            if k & bit:
                to = to + bit - 2 * bit * lax.rem(lax.div(me, bit), 2)
            bit *= 2
        return to

    if groups & (groups - 1):
        targets = [lax.rem(me + k, groups) for k in range(1, groups)]
    else:
        targets = [partner_at(k) for k in range(groups - 1, 0, -1)]

    @pl.when(me == 0)
    def _():
        for b in range(blocks):
            for source in range(groups):
                back[0, b, source, 1] = jnp.zeros(back.shape[4:], BF16)

    def lesser_step(j, carry):
        own[0], own[1] = sandwich(gd[j, 0], gd[j, 1], -gd[j, 1], sig[j, 0], sig[j, 1])
        minus[...] = -gu[j, 1]
        wminus[j] = -scr[j, 1]

        def pack(re, im):
            for c, part in enumerate((re, im)):
                value = part.astype(BF16).reshape(size // SUB, SUB, size)
                for b in range(blocks):
                    lbuf[j, b, :, c] = value[b * groups : (b + 1) * groups]
                for i in range(cores * extra):
                    lred[j, i // extra, i % extra, c] = value[blocks * groups + i]

        @pl.when(cut < slices - 1)
        def _():
            shift_mine(j).wait_recv()
            shift_loan(j).wait_recv()
            re, im = sandwich(gu[j, 0], gu[j, 1], minus[...], snext[j, 0], snext[j, 1])
            pack(own[0] + re, own[1] + im)

        @pl.when(cut == slices - 1)
        def _():
            pack(own[0], own[1])

        @pl.when((j == 0) & (me > 0))
        def _():
            pl.semaphore_wait(go, 1)

        def spread(b):
            def send(to):
                pltpu.make_async_remote_copy(
                    src_ref=lbuf.at[j, b, to], dst_ref=ents.at[j, b, me],
                    send_sem=a_send.at[j, b], recv_sem=a_recv.at[j, b],
                    device_id={"energy": to}, device_id_type=MESH,
                ).start()

            for to in targets:
                send(to)
            ents[j, b, me] = lbuf[j, b, me]

        def spread_whole():
            for to in targets:
                pltpu.make_async_remote_copy(
                    src_ref=lbuf.at[j, :, to], dst_ref=ents.at[j, :, me],
                    send_sem=a_send.at[j, 0], recv_sem=a_recv.at[j, 0],
                    device_id={"energy": to}, device_id_type=MESH,
                ).start()
            for b in range(blocks):
                ents[j, b, me] = lbuf[j, b, me]

        pl.when(j < last)(spread_whole)
        pl.when(j == last)(lambda: each(blocks, spread))

        def send_extra(to):
            pltpu.make_async_remote_copy(
                src_ref=lred.at[j, lax.rem(to, cores)], dst_ref=entr.at[j, me],
                send_sem=r_send.at[j], recv_sem=r_recv.at[j],
                device_id={"energy": to}, device_id_type=MESH,
            ).start()

        if extra:
            for to in targets:
                send_extra(to)
            entr[j, me] = lred[j, lax.rem(me, cores)]
        @pl.when(j > 0)
        def _():
            whole = ents.at[j - 1, :, pl.ds(0, groups - 1)]
            pltpu.make_async_copy(whole, whole, a_recv.at[j - 1, 0]).wait()
            each(blocks, lambda b: forward(b, j - 1, ents[j - 1, b]))
            if extra:
                wait_for(entr.at[j - 1], r_recv.at[j - 1])
                each(extra, lambda i: forward(blocks + i, j - 1, entr[j - 1, :, i]))

        return carry

    lax.fori_loop(0, local, lesser_step, 0)

    slots = [u if 2 * u <= local else local - u for u in range(local)]
    offset = [max(0, 2 * u - 1) for u in range(local // 2 + 1)]

    def spectrum(block):
        step = 2 * SUB
        for at in range(0, half, step):
            for lane in range(0, size, LANES):
                lanes = slice(lane, lane + LANES)
                z = [
                    (zbuf[block, j, at : at + step, lanes], zbuf[block, j, half + at : half + at + step, lanes])
                    for j in range(local)
                ]
                power = [(re * re + im * im, None) for re, im in short_transform(z, -1)]
                for u, (re, im) in enumerate(short_transform(power, 1)[: local // 2 + 1]):
                    qbuf[offset[u], at : at + step, lanes] = re.astype(BF16)
                    if 0 < 2 * u < local:
                        qbuf[offset[u] + 1, at : at + step, lanes] = im.astype(BF16)

    def lags(u, rows):
        slot = slots[u]
        if 0 < 2 * slot < local:
            q = qbuf[offset[slot] : offset[slot] + 2].reshape(2 * half, size)
            return dot(inv_ref[u, rows, :], q)
        return dot(inv_ref[u, rows, :half], qbuf[offset[slot]])

    def hand_over():
        return pltpu.make_async_remote_copy(
            src_ref=rbuf, dst_ref=redp.at[first],
            send_sem=d_sem.at[0], recv_sem=d_sem.at[1],
            device_id={"energy": partner}, device_id_type=MESH,
        )

    def shared_rows():
        wait_for(entr.at[last], r_recv.at[last])

        def extra_step(i, carry):
            forward(blocks + i, last, entr[last, :, i])
            spectrum(blocks + i)
            step = 2 * SUB
            for u in range(local):
                mine = lags(u, pl.ds(pl.multiple_of(me * step, step), step))
                theirs = lags(u, pl.ds(pl.multiple_of(partner * step, step), step))
                redp[first, u, i] = mine.reshape(2, SUB, size).astype(BF16)
                rbuf[u, i] = theirs.reshape(2, SUB, size).astype(BF16)
            return carry

        lax.fori_loop(0, extra, extra_step, 0)
        hand_over().start()

    def block_step(b, carry):
        if extra:
            pl.when(b == blocks - 1)(shared_rows)

        forward_block(last, b)
        spectrum(b)
        for u in range(local):
            pbuf[b, u] = lags(u, slice(None)).reshape(groups, 2, SUB, size).astype(BF16)

            def send(to):
                pltpu.make_async_remote_copy(
                    src_ref=pbuf.at[b, u, to], dst_ref=back.at[u, b, me],
                    send_sem=b_send.at[b, u], recv_sem=b_recv.at[b, u],
                    device_id={"energy": to}, device_id_type=MESH,
                ).start()

            def send_real():
                pltpu.make_async_remote_copy(
                    src_ref=pbuf.at[b, 0, 0, 0], dst_ref=back.at[0, b, me, 0],
                    send_sem=b_real.at[0, b], recv_sem=b_real.at[1, b],
                    device_id={"energy": 0}, device_id_type=MESH,
                ).start()

            for to in targets:
                if u:
                    send(to)
                else:
                    pl.when(to > 0)(functools.partial(send, to))
                    pl.when(to == 0)(send_real)
            back[u, b, me] = pbuf[b, u, me]
        return carry

    lax.fori_loop(0, blocks, block_step, 0)

    @pl.when(cut > 0)
    def _():
        for j in range(local):
            shift_mine(j).wait_send()
            shift_loan(j).wait_send()
            lend(j).wait_send()

    for j in range(local):
        if extra:
            wait_for(entr.at[j], r_send.at[j])
        if j < last:
            whole = lbuf.at[j, :, pl.ds(0, groups - 1)]
            pltpu.make_async_copy(whole, whole, a_send.at[j, 0]).wait()
            continue
        for b in range(blocks):
            wait_for(lbuf.at[j, b], a_send.at[j, b])

    def sent(b):
        for j in range(1, local):
            wait_for(pbuf.at[b, j], b_send.at[b, j])

        @pl.when(me == 0)
        def _():
            wait_for(pbuf.at[b, 0], b_send.at[b, 0])

        @pl.when(me > 0)
        def _():
            other = pbuf.at[b, 0, pl.ds(0, groups - 2)]
            pltpu.make_async_copy(other, other, b_send.at[b, 0]).wait()
            real = pbuf.at[b, 0, 0, 0]
            pltpu.make_async_copy(real, real, b_real.at[0, b]).wait()

    ahead = blocks - 1
    depth = ahead * groups * SUB
    if depth % LANES:
        ahead = depth = 0

    def returned(u, some):
        real_only = (me == 0) & (u == 0)

        @pl.when(real_only)
        def _():
            for b in some:
                wait_for(back.at[0, b, :, 0], b_real.at[1, b])

        @pl.when(jnp.logical_not(real_only))
        def _():
            for b in some:
                wait_for(back.at[u, b], b_recv.at[b, u])

    def screen(u, columns):
        return scr[u, 0, :, columns], scr[u, 1, :, columns], wminus[u, :, columns]

    def early_product(u):
        returned(u, range(ahead))
        polar = [back[u, :ahead, :, c].reshape(depth, size) for c in range(2)]
        part[u, 0], part[u, 1] = product(*screen(u, slice(0, depth)), *polar)

    if ahead:
        each(local, early_product)

    for b in range(blocks - 1):
        sent(b)
    if extra:
        hand_over().wait_send()
        hand_over().wait_recv()

    def result_step(u, carry):
        returned(u, range(ahead, blocks))
        polar = []
        for c in range(2):
            value = back[u, ahead:, :, c].reshape((blocks - ahead) * groups * SUB, size)
            if extra:
                value = above(value, redp[:, u, :, c].reshape(cores * extra * SUB, size))
            polar.append(value)
        tr, ti = product(*screen(u, slice(depth, size)), *polar)
        if ahead:
            tr, ti = part[u, 0] + tr, part[u, 1] + ti
        re, im = adjoint_product(tr, ti, scr[u, 0], scr[u, 1], wminus[u])
        out_ref[u, 0] = re.astype(BF16)
        out_ref[u, 1] = im.astype(BF16)
        return carry

    lax.fori_loop(0, local, result_step, 0)

    sent(blocks - 1)


def solution(mesh):
    groups, slices = mesh.shape["energy"], mesh.shape["cuts"]
    cores = 2

    def shards(green_diag, green_upper, sigma_lesser, screening):
        shape = green_diag.shape[1:]
        local, _, size, _ = shape
        shared = size // SHARE
        if (size - shared) % (groups * SUB) or shared % (cores * SUB):
            shared = 0
        blocks = (size - shared) // (groups * SUB)
        extra = shared // (cores * SUB)
        some = max(1, extra)
        half = 2 * groups * SUB
        tile = (2, SUB, size)
        block = pltpu.VMEM(shape, BF16)
        dma = pltpu.SemaphoreType.DMA
        anywhere = pl.BlockSpec(memory_space=pltpu.HBM)
        result = pl.pallas_call(
            functools.partial(kernel, groups, slices, cores),
            out_shape=jax.ShapeDtypeStruct(shape, BF16),
            in_specs=[anywhere] * 4,
            out_specs=pl.BlockSpec(memory_space=pltpu.VMEM),
            scratch_shapes=[
                pltpu.VMEM((local, 2 * half, half), BF16),
                pltpu.VMEM((local, half, 2 * half), BF16),
                block, block, block, block, block,
                pltpu.VMEM((local,) + shape[2:], BF16),
                pltpu.VMEM(shape[1:], F32),
                pltpu.VMEM(shape, F32),
                pltpu.VMEM(shape[2:], BF16),
                pltpu.VMEM((local,) + shape[2:], BF16),
                pltpu.VMEM((local, blocks, groups) + tile, BF16),
                pltpu.VMEM((local, cores, some) + tile, BF16),
                pltpu.VMEM((local, blocks, groups) + tile, BF16),
                pltpu.VMEM((local, groups, some) + tile, BF16),
                pltpu.VMEM((blocks + extra, local, 2 * half, size), F32),
                pltpu.VMEM((local, half, size), BF16),
                pltpu.VMEM((blocks, local, groups) + tile, BF16),
                pltpu.VMEM((local, blocks, groups) + tile, BF16),
                pltpu.VMEM((local, some) + tile, BF16),
                pltpu.VMEM((cores, local, some) + tile, BF16),
                pltpu.SemaphoreType.REGULAR, pltpu.SemaphoreType.REGULAR,
                dma((4,)),
                dma((2, local)), dma((2, local)), dma((local,)), dma((local,)),
                dma((local, blocks)), dma((local, blocks)), dma((local,)), dma((local,)),
                dma((blocks, local)), dma((blocks, local)), dma((2, blocks)), dma((2,)),
            ],
            compiler_params=pltpu.CompilerParams(
                collective_id=0, has_side_effects=True, vmem_limit_bytes=54525952
            ),
        )(
            green_diag[0], green_upper[0], sigma_lesser[0], screening[0]
        )
        return result[None]

    spec = P("cuts", "energy", None, None, None)
    return jax.shard_map(
        shards, mesh=mesh, in_specs=(spec,) * 4, out_specs=spec, check_vma=False
    )
```

```python
import functools
import math

import jax
import jax.numpy as jnp
from jax import lax
from jax.experimental import pallas as pl
from jax.experimental.pallas import tpu as pltpu
from jax.sharding import PartitionSpec as P

LANES = 128
SUB = 8
SHARE = 4
MESH = pl.DeviceIdType.MESH
F32 = jnp.float32
BF16 = jnp.bfloat16


def fill_tables(fwd_ref, inv_ref, groups, local):
    width = 2 * groups
    period = width * local
    side = max(LANES, 2 * width)

    def index(shape, axis, unit=1, count=None):
        value = lax.div(lax.broadcasted_iota(jnp.int32, shape, axis), unit)
        return value if count is None else lax.rem(value, count)

    def table(phase, quarters, scale):
        turn = lax.rem(phase + quarters * (period // 4), period)
        return (jnp.cos(turn.astype(F32) * (2.0 * math.pi / period)) * scale).astype(BF16)

    def ones(condition):
        return jnp.where(condition, 1.0, 0.0).astype(BF16)

    small = (side, side)

    def expander(shape):
        tall, wide = (shape[0], side), (side, shape[1])
        left = ones(index(tall, 0, SUB) == index(tall, 1))
        right = ones(index(wide, 0) == index(wide, 1, SUB))
        same = index(shape, 0, 1, SUB) == index(shape, 1, 1, SUB)

        def expand(value):
            spread = dot(dot(left, value).astype(BF16), right)
            return jnp.where(same, spread, 0.0).astype(BF16)

        return expand

    expand = expander(fwd_ref.shape[1:])
    for j in range(local):
        point = index(small, 0, 1, width)
        turn = index(small, 0, width, 2) - index(small, 1, 1, 2) + 4
        energy = index(small, 1, 2, groups) * local + j
        fwd_ref[j] = expand(table(lax.rem(point * energy, period), turn, 1.0))

    expand = expander(inv_ref.shape[1:])
    for j in range(local):
        component = index(small, 0, 1, 2)
        part = index(small, 1, width, 2)
        lag = index(small, 0, 2, groups) * local + j
        other = 1 - component if 2 * j <= local else 3 - component
        turn = jnp.where(part == 0, 3 * component, other)
        point = index(small, 1, 1, width)
        inv_ref[j] = expand(table(lax.rem(point * lag, period), turn, 2.0 / period / period))


def negated(x):
    return None if x is None else -x


def scaled(x, factor):
    return None if x is None else x * factor


def turned(value, numerator, denominator):
    re, im = value
    angle = numerator % denominator
    if angle == 0:
        return re, im
    if 2 * angle == denominator:
        return negated(re), negated(im)
    if 4 * angle == denominator:
        return negated(im), re
    if 4 * angle == 3 * denominator:
        return im, negated(re)
    c = math.cos(2.0 * math.pi * angle / denominator)
    s = math.sin(2.0 * math.pi * angle / denominator)
    return added((scaled(re, c), scaled(re, s)), (scaled(im, -s), scaled(im, c)))


def added(left, right):
    def one(x, y):
        return y if x is None else x if y is None else x + y

    return one(left[0], right[0]), one(left[1], right[1])


def short_transform(values, sign):
    count = len(values)
    if count == 1:
        return values
    if count % 2:
        result = []
        for m in range(count):
            total = values[0]
            for j in range(1, count):
                total = added(total, turned(values[j], sign * j * m, count))
            result.append(total)
        return result
    even = short_transform(values[0::2], sign)
    odd = short_transform(values[1::2], sign)
    half = count // 2
    odd = [turned(value, sign * m, count) for m, value in enumerate(odd)]
    minus = [turned(value, 1, 2) for value in odd]
    return [added(e, o) for e, o in zip(even, odd)] + [added(e, o) for e, o in zip(even, minus)]


def dot(left, right):
    return jnp.dot(left, right, preferred_element_type=F32)


def dot_t(left, right):
    return lax.dot_general(left, right, (((1,), (1,)), ((), ())), preferred_element_type=F32)


def beside(left, right):
    return jnp.concatenate([left, right], axis=1)


def above(top, bottom):
    return jnp.concatenate([top, bottom], axis=0)


def product(re, im, negative, middle_re, middle_im):
    middle = above(middle_re, middle_im)
    return dot(beside(re, negative), middle), dot(beside(im, re), middle)


def adjoint_product(tr, ti, re, im, negative):
    left = beside(tr.astype(BF16), ti.astype(BF16))
    return dot_t(left, beside(re, im)), dot_t(left, beside(negative, re))


def sandwich(re, im, negative, middle_re, middle_im):
    tr, ti = product(re, im, negative, middle_re, middle_im)
    return adjoint_product(tr, ti, re, im, negative)


def kernel(
    groups, slices, cores,
    gd_hbm, gu_hbm, s_hbm, w_hbm, out_ref,
    fwd_ref, inv_ref, gd, gu, sig, scr, snext, loan, own, part, minus, wminus,
    lbuf, lred, ents, entr, zbuf, qbuf, pbuf, back, rbuf, redp,
    ready, go, in_sem, z_send, z_recv, l_send, l_recv, a_send, a_recv, r_send, r_recv, b_send, b_recv, b_real, d_sem,
):
    me = lax.axis_index("energy")
    cut = lax.axis_index("cuts")
    local, _, size, _ = gd.shape
    blocks = lbuf.shape[1]
    extra = (size // SUB - blocks * groups) // cores

    barrier = pltpu.get_barrier_semaphore()

    first = lax.rem(me, 2)
    partner = me + 1 - 2 * first
    last = local - 1

    @pl.when(cut < slices - 1)
    def _():
        for who in (me, partner):
            pl.semaphore_signal(
                barrier, inc=1, device_id={"energy": who, "cuts": cut + 1}, device_id_type=MESH
            )

    pl.semaphore_signal(barrier, inc=1, device_id={"energy": partner}, device_id_type=MESH)

    def to_others(semaphore):
        def greet(k, carry):
            pl.semaphore_signal(semaphore, inc=1, device_id={"energy": k}, device_id_type=MESH)
            return carry

        lax.fori_loop(1, groups, greet, 0)

    @pl.when(me == 0)
    def _():
        to_others(barrier)

    loads = [
        pltpu.make_async_copy(source, target, in_sem.at[i])
        for i, (source, target) in enumerate(
            [(gd_hbm, gd), (s_hbm, sig), (gu_hbm, gu), (w_hbm, scr)]
        )
    ]
    pl.semaphore_wait(
        barrier, 1 + jnp.where(me > 0, 1, 0) + 2 * jnp.where(cut > 0, 1, 0)
    )

    def lend(j):
        return pltpu.make_async_remote_copy(
            src_ref=s_hbm.at[j, 1 - first], dst_ref=loan.at[j],
            send_sem=l_send.at[j], recv_sem=l_recv.at[j],
            device_id={"energy": partner, "cuts": cut}, device_id_type=MESH,
        )

    def shift_mine(j):
        return pltpu.make_async_remote_copy(
            src_ref=s_hbm.at[j, first], dst_ref=snext.at[j, first],
            send_sem=z_send.at[0, j], recv_sem=z_recv.at[0, j],
            device_id={"energy": me, "cuts": cut - 1}, device_id_type=MESH,
        )

    def shift_loan(j):
        return pltpu.make_async_remote_copy(
            src_ref=loan.at[j], dst_ref=snext.at[j, first],
            send_sem=z_send.at[1, j], recv_sem=z_recv.at[1, j],
            device_id={"energy": partner, "cuts": cut - 1}, device_id_type=MESH,
        )

    @pl.when(cut > 0)
    def _():
        shift_mine(0).start()
        for j in range(local):
            lend(j).start()
        lend(0).wait_recv()
        shift_loan(0).start()

        @pl.when(first == 0)
        def _():
            for j in range(1, local):
                shift_mine(j).start()
                lend(j).wait_recv()
                shift_loan(j).start()

        @pl.when(first == 1)
        def _():
            for j in range(1, local):
                lend(j).wait_recv()
                shift_loan(j).start()
                shift_mine(j).start()

    for load in loads:
        load.start()

    @pl.when(me > 0)
    def _():
        pl.semaphore_signal(ready, inc=1, device_id={"energy": 0}, device_id_type=MESH)

    @pl.when(me == 0)
    def _():
        pl.semaphore_wait(ready, groups - 1)
        to_others(go)

    fill_tables(fwd_ref, inv_ref, groups, local)
    for load in loads:
        load.wait()

    half = 2 * groups * SUB

    def forward(at, j, entries):
        zbuf[at, j] = dot(fwd_ref[j], entries.reshape(half, size))

    def forward_block(j, b):
        wait_for(ents.at[j, b], a_recv.at[j, b])
        forward(b, j, ents[j, b])

    def wait_for(some, semaphore):
        landed = some.at[pl.ds(0, groups - 1)]
        pltpu.make_async_copy(landed, landed, semaphore).wait()

    def each(count, body):
        lax.fori_loop(0, count, lambda b, carry: (body(b), carry)[1], 0)

    def partner_at(k):
        to = me
        bit = 1
        while bit < groups:
            if k & bit:
                to = to + bit - 2 * bit * lax.rem(lax.div(me, bit), 2)
            bit *= 2
        return to

    if groups & (groups - 1):
        targets = [lax.rem(me + k, groups) for k in range(1, groups)]
    else:
        targets = [partner_at(k) for k in range(groups - 1, 0, -1)]

    @pl.when(me == 0)
    def _():
        for b in range(blocks):
            for source in range(groups):
                back[0, b, source, 1] = jnp.zeros(back.shape[4:], BF16)

    def lesser_step(j, carry):
        own[0], own[1] = sandwich(gd[j, 0], gd[j, 1], -gd[j, 1], sig[j, 0], sig[j, 1])
        minus[...] = -gu[j, 1]
        wminus[j] = -scr[j, 1]

        def pack(re, im):
            for c, part in enumerate((re, im)):
                value = part.astype(BF16).reshape(size // SUB, SUB, size)
                for b in range(blocks):
                    lbuf[j, b, :, c] = value[b * groups : (b + 1) * groups]
                for i in range(cores * extra):
                    lred[j, i // extra, i % extra, c] = value[blocks * groups + i]

        @pl.when(cut < slices - 1)
        def _():
            shift_mine(j).wait_recv()
            shift_loan(j).wait_recv()
            re, im = sandwich(gu[j, 0], gu[j, 1], minus[...], snext[j, 0], snext[j, 1])
            pack(own[0] + re, own[1] + im)

        @pl.when(cut == slices - 1)
        def _():
            pack(own[0], own[1])

        @pl.when((j == 0) & (me > 0))
        def _():
            pl.semaphore_wait(go, 1)

        def spread(b):
            def send(to):
                pltpu.make_async_remote_copy(
                    src_ref=lbuf.at[j, b, to], dst_ref=ents.at[j, b, me],
                    send_sem=a_send.at[j, b], recv_sem=a_recv.at[j, b],
                    device_id={"energy": to}, device_id_type=MESH,
                ).start()

            for to in targets:
                send(to)
            ents[j, b, me] = lbuf[j, b, me]

        each(blocks, spread)

        def send_extra(to):
            pltpu.make_async_remote_copy(
                src_ref=lred.at[j, lax.rem(to, cores)], dst_ref=entr.at[j, me],
                send_sem=r_send.at[j], recv_sem=r_recv.at[j],
                device_id={"energy": to}, device_id_type=MESH,
            ).start()

        if extra:
            for to in targets:
                send_extra(to)
            entr[j, me] = lred[j, lax.rem(me, cores)]
        @pl.when(j > 0)
        def _():
            each(blocks, lambda b: forward_block(j - 1, b))
            if extra:
                wait_for(entr.at[j - 1], r_recv.at[j - 1])
                each(extra, lambda i: forward(blocks + i, j - 1, entr[j - 1, :, i]))

        return carry

    lax.fori_loop(0, local, lesser_step, 0)

    slots = [u if 2 * u <= local else local - u for u in range(local)]
    offset = [max(0, 2 * u - 1) for u in range(local // 2 + 1)]

    def spectrum(block):
        step = 2 * SUB
        for at in range(0, half, step):
            for lane in range(0, size, LANES):
                lanes = slice(lane, lane + LANES)
                z = [
                    (zbuf[block, j, at : at + step, lanes], zbuf[block, j, half + at : half + at + step, lanes])
                    for j in range(local)
                ]
                power = [(re * re + im * im, None) for re, im in short_transform(z, -1)]
                for u, (re, im) in enumerate(short_transform(power, 1)[: local // 2 + 1]):
                    qbuf[offset[u], at : at + step, lanes] = re.astype(BF16)
                    if 0 < 2 * u < local:
                        qbuf[offset[u] + 1, at : at + step, lanes] = im.astype(BF16)

    def lags(u, rows):
        slot = slots[u]
        if 0 < 2 * slot < local:
            q = qbuf[offset[slot] : offset[slot] + 2].reshape(2 * half, size)
            return dot(inv_ref[u, rows, :], q)
        return dot(inv_ref[u, rows, :half], qbuf[offset[slot]])

    def hand_over():
        return pltpu.make_async_remote_copy(
            src_ref=rbuf, dst_ref=redp.at[first],
            send_sem=d_sem.at[0], recv_sem=d_sem.at[1],
            device_id={"energy": partner}, device_id_type=MESH,
        )

    def shared_rows():
        wait_for(entr.at[last], r_recv.at[last])

        def extra_step(i, carry):
            forward(blocks + i, last, entr[last, :, i])
            spectrum(blocks + i)
            step = 2 * SUB
            for u in range(local):
                mine = lags(u, pl.ds(pl.multiple_of(me * step, step), step))
                theirs = lags(u, pl.ds(pl.multiple_of(partner * step, step), step))
                redp[first, u, i] = mine.reshape(2, SUB, size).astype(BF16)
                rbuf[u, i] = theirs.reshape(2, SUB, size).astype(BF16)
            return carry

        lax.fori_loop(0, extra, extra_step, 0)
        hand_over().start()

    def block_step(b, carry):
        if extra:
            pl.when(b == blocks - 1)(shared_rows)

        forward_block(last, b)
        spectrum(b)
        def make(u):
            pbuf[b, u] = lags(u, slice(None)).reshape(groups, 2, SUB, size).astype(BF16)
            back[u, b, me] = pbuf[b, u, me]

        def send(u, to):
            pltpu.make_async_remote_copy(
                src_ref=pbuf.at[b, u, to], dst_ref=back.at[u, b, me],
                send_sem=b_send.at[b, u], recv_sem=b_recv.at[b, u],
                device_id={"energy": to}, device_id_type=MESH,
            ).start()

        def send_real():
            pltpu.make_async_remote_copy(
                src_ref=pbuf.at[b, 0, 0, 0], dst_ref=back.at[0, b, me, 0],
                send_sem=b_real.at[0, b], recv_sem=b_real.at[1, b],
                device_id={"energy": 0}, device_id_type=MESH,
            ).start()

        make(0)
        for u in range(local):
            if u < last:
                make(u + 1)
            for to in targets:
                near = to < cores
                if u == 0:
                    pl.when(to == 0)(send_real)
                    pl.when(near & (to > 0))(functools.partial(send, 0, to))
                if u < last:
                    send(u + jnp.where(near, 1, 0), to)
                else:
                    pl.when(jnp.logical_not(near))(functools.partial(send, u, to))
        return carry

    lax.fori_loop(0, blocks, block_step, 0)

    @pl.when(cut > 0)
    def _():
        for j in range(local):
            shift_mine(j).wait_send()
            shift_loan(j).wait_send()
            lend(j).wait_send()

    for j in range(local):
        if extra:
            wait_for(entr.at[j], r_send.at[j])
        for b in range(blocks):
            wait_for(lbuf.at[j, b], a_send.at[j, b])

    def sent(b):
        for j in range(1, local):
            wait_for(pbuf.at[b, j], b_send.at[b, j])

        @pl.when(me == 0)
        def _():
            wait_for(pbuf.at[b, 0], b_send.at[b, 0])

        @pl.when(me > 0)
        def _():
            other = pbuf.at[b, 0, pl.ds(0, groups - 2)]
            pltpu.make_async_copy(other, other, b_send.at[b, 0]).wait()
            real = pbuf.at[b, 0, 0, 0]
            pltpu.make_async_copy(real, real, b_real.at[0, b]).wait()

    ahead = blocks - 1
    depth = ahead * groups * SUB
    if depth % LANES:
        ahead = depth = 0

    def returned(u, some):
        real_only = (me == 0) & (u == 0)

        @pl.when(real_only)
        def _():
            for b in some:
                wait_for(back.at[0, b, :, 0], b_real.at[1, b])

        @pl.when(jnp.logical_not(real_only))
        def _():
            for b in some:
                wait_for(back.at[u, b], b_recv.at[b, u])

    def screen(u, columns):
        return scr[u, 0, :, columns], scr[u, 1, :, columns], wminus[u, :, columns]

    def early_product(u):
        returned(u, range(ahead))
        polar = [back[u, :ahead, :, c].reshape(depth, size) for c in range(2)]
        part[u, 0], part[u, 1] = product(*screen(u, slice(0, depth)), *polar)

    if ahead:
        each(local, early_product)

    for b in range(blocks - 1):
        sent(b)
    if extra:
        hand_over().wait_send()
        hand_over().wait_recv()

    def result_step(u, carry):
        returned(u, range(ahead, blocks))
        polar = []
        for c in range(2):
            value = back[u, ahead:, :, c].reshape((blocks - ahead) * groups * SUB, size)
            if extra:
                value = above(value, redp[:, u, :, c].reshape(cores * extra * SUB, size))
            polar.append(value)
        tr, ti = product(*screen(u, slice(depth, size)), *polar)
        if ahead:
            tr, ti = part[u, 0] + tr, part[u, 1] + ti
        re, im = adjoint_product(tr, ti, scr[u, 0], scr[u, 1], wminus[u])
        out_ref[u, 0] = re.astype(BF16)
        out_ref[u, 1] = im.astype(BF16)
        return carry

    lax.fori_loop(0, local, result_step, 0)

    sent(blocks - 1)


def solution(mesh):
    groups, slices = mesh.shape["energy"], mesh.shape["cuts"]
    cores = 2

    def shards(green_diag, green_upper, sigma_lesser, screening):
        shape = green_diag.shape[1:]
        local, _, size, _ = shape
        shared = size // SHARE
        if (size - shared) % (groups * SUB) or shared % (cores * SUB):
            shared = 0
        blocks = (size - shared) // (groups * SUB)
        extra = shared // (cores * SUB)
        some = max(1, extra)
        half = 2 * groups * SUB
        tile = (2, SUB, size)
        block = pltpu.VMEM(shape, BF16)
        dma = pltpu.SemaphoreType.DMA
        anywhere = pl.BlockSpec(memory_space=pltpu.HBM)
        result = pl.pallas_call(
            functools.partial(kernel, groups, slices, cores),
            out_shape=jax.ShapeDtypeStruct(shape, BF16),
            in_specs=[anywhere] * 4,
            out_specs=pl.BlockSpec(memory_space=pltpu.VMEM),
            scratch_shapes=[
                pltpu.VMEM((local, 2 * half, half), BF16),
                pltpu.VMEM((local, half, 2 * half), BF16),
                block, block, block, block, block,
                pltpu.VMEM((local,) + shape[2:], BF16),
                pltpu.VMEM(shape[1:], F32),
                pltpu.VMEM(shape, F32),
                pltpu.VMEM(shape[2:], BF16),
                pltpu.VMEM((local,) + shape[2:], BF16),
                pltpu.VMEM((local, blocks, groups) + tile, BF16),
                pltpu.VMEM((local, cores, some) + tile, BF16),
                pltpu.VMEM((local, blocks, groups) + tile, BF16),
                pltpu.VMEM((local, groups, some) + tile, BF16),
                pltpu.VMEM((blocks + extra, local, 2 * half, size), F32),
                pltpu.VMEM((local, half, size), BF16),
                pltpu.VMEM((blocks, local, groups) + tile, BF16),
                pltpu.VMEM((local, blocks, groups) + tile, BF16),
                pltpu.VMEM((local, some) + tile, BF16),
                pltpu.VMEM((cores, local, some) + tile, BF16),
                pltpu.SemaphoreType.REGULAR, pltpu.SemaphoreType.REGULAR,
                dma((4,)),
                dma((2, local)), dma((2, local)), dma((local,)), dma((local,)),
                dma((local, blocks)), dma((local, blocks)), dma((local,)), dma((local,)),
                dma((blocks, local)), dma((blocks, local)), dma((2, blocks)), dma((2,)),
            ],
            compiler_params=pltpu.CompilerParams(
                collective_id=0, has_side_effects=True, vmem_limit_bytes=54525952
            ),
        )(
            green_diag[0], green_upper[0], sigma_lesser[0], screening[0]
        )
        return result[None]

    spec = P("cuts", "energy", None, None, None)
    return jax.shard_map(
        shards, mesh=mesh, in_specs=(spec,) * 4, out_specs=spec, check_vma=False
    )
```
